32 devices in a mesh: lat: 4 (over x, core), lon: 8 (over z, y).
Axes of the slice: x: 2, y: 2, z: 4, core: 2. Of those that a mesh axis runs over, the one named last changes fastest.
Arguments:
- ensemble: bfloat16 [1920, 32, 1024], P(('lat', 'lon')), may hold values from -48 to 48
- obs_interp: bfloat16 [4, 8, 64, 4, 128], P('lat', 'lon'), may hold values from 0.049804688 to 1
- obs_start: int32 [4, 8, 64, 128], P('lat', 'lon'), may hold values from 0 to 124
- obs_levels: bfloat16 [4, 8, 64, 24, 128], P('lat', 'lon'), may hold values from -1.25 to 1.25
- obs_values: float32 [4, 8, 64, 128], P('lat', 'lon'), may hold values from -40 to 40
- obs_weight: float32 [4, 8, 64, 128], P('lat', 'lon'), may hold values from 0.001953125 to 0.00390625
- obs_rows: int32 [4, 8, 64], P('lat', 'lon'), may hold values from 0 to 7
- obs_count: int32 [4, 8], P('lat', 'lon'), may hold values from 8 to 64, as said below
- local_mask: int32 [4, 8, 8, 9], P('lat', 'lon'), may hold values 0 or 1
Outputs:
- analysis: bfloat16 [80, 24, 32, 1024], P(None, None, 'lat', 'lon')
The draws below stay inside these ranges and needn't reach their ends.
Inputs may be any that keep to these rules, and one draw needn't show every extreme that they name: `obs_count`: blocks from this slot on are ignored; some tile has 64 live blocks.
All inputs are finite; a program needn't handle non-finite values. No bound on the sum of `local_mask` on one device may be relied on, other than what follows from the above.
Results may differ from the reference program's by a relative error of at most 0.005.
Values may be sent and summed in bfloat16 or wider, within the bound.
A program may use at most 64 MiB of HBM per device.

```python
import math
import jax
import jax.numpy as jnp
from jax import lax

K = 80
NF = 24
TLAT = 8
TLON = 128
OB = 128
STENCIL = 4
MAXB = 64
NS_ITERS = 6
LAT_TILES = 4
LON_TILES = 8
NY = 32
NX = 1024


def draw_ensemble(key, part):
    keys = jax.random.split(key, 3)
    common = jax.random.normal(keys[0], (NF, NY, NX), jnp.float32)
    spread = jnp.exp(jax.random.uniform(keys[1], (K, 1, 1, 1), jnp.float32, jnp.log(0.5), jnp.log(4.0)))
    noise = jax.random.normal(keys[2], (K, NF, NY, NX), jnp.float32)
    return (common[None] + spread * noise).reshape(K * NF, NY, NX).astype(jnp.bfloat16)


def draw_obs_count(key, part):
    keys = jax.random.split(key, 4)
    tile_total = LAT_TILES * LON_TILES
    lowest = MAXB // 8
    drawn = jax.random.randint(keys[0], (tile_total,), lowest, MAXB // 2 + 1)
    dense = jax.random.randint(keys[1], (tile_total,), 0, 8) == 0
    heavy = jax.random.randint(keys[2], (tile_total,), 3 * MAXB // 4, MAXB + 1)
    counts = jnp.where(dense, heavy, drawn)
    order = jax.random.permutation(keys[3], tile_total)
    counts = counts.at[order[0]].set(MAXB).at[order[1]].set(lowest)
    return counts.reshape(LAT_TILES, LON_TILES).astype(jnp.int32)


def touch_ends(array, own_key, low, largest):
    longest = array.shape.index(max(array.shape))
    spots = []
    for shift in (0, 1):
        where = [jax.random.randint(jax.random.fold_in(own_key, axis), (), 0, length) for axis, length in enumerate(array.shape)]
        where[longest] = (where[longest] + shift) % array.shape[longest]
        spots.append(tuple(where))
    return array.at[spots[0]].set(low).at[spots[1]].set(largest)


def steps_of(rng, extent, shards, least, top_value):
    def one(axis_at, blocks):
        draws = jax.random.uniform(jax.random.fold_in(jax.random.fold_in(rng, 6), axis_at), (blocks,), jnp.float32, least / len(shards), top_value / len(shards))
        return jnp.repeat(jnp.exp(draws), extent[axis_at] // blocks).reshape((-1,) + (1,) * (len(extent) - axis_at - 1))

    gain = one(*shards[0])
    for cut in shards[1:]:
        gain = gain * one(*cut)
    return gain


def centred(own_key, extent, scale, most, cuts=(), kind=jnp.bfloat16):
    gain = steps_of(own_key, extent, cuts, -0.22, 0.18) if cuts else 1.0
    values = jax.random.normal(own_key, extent, jnp.float32) * scale * gain
    return jnp.minimum(jnp.maximum(values, -most), most).astype(kind)


def setup_inputs(seed: int = 0) -> dict:
    streams_of = jax.random.split(jax.random.key(seed), 10)
    return {
        "ensemble": draw_ensemble(jax.random.fold_in(streams_of[9], 71), 0),
        "obs_interp": jnp.clip(0.049804688 + 0.9501953 * jax.random.uniform(streams_of[1], (LAT_TILES, LON_TILES, MAXB, STENCIL, OB), jnp.float32) ** steps_of(streams_of[1], (LAT_TILES, LON_TILES, MAXB, STENCIL, OB), ((0, 4), (1, 8)), -0.2, 0.2), 0.049804688, 1.0).astype(jnp.bfloat16),
        "obs_start": touch_ends(jax.random.randint(streams_of[2], (LAT_TILES, LON_TILES, MAXB, OB), 0, TLON - STENCIL + 1), jax.random.fold_in(streams_of[2], 1), 0, TLON - STENCIL).astype(jnp.int32),
        "obs_levels": centred(streams_of[3], (LAT_TILES, LON_TILES, MAXB, NF, OB), NF ** -0.5, 1.25, ((0, 4), (1, 8))),
        "obs_values": centred(streams_of[4], (LAT_TILES, LON_TILES, MAXB, OB), 8.0, 40.0, ((0, 4), (1, 8)), jnp.float32),
        "obs_weight": jnp.clip(jnp.exp(math.log(0.00390625) - 0.6931472 * jax.random.uniform(streams_of[5], (LAT_TILES, LON_TILES, MAXB, OB), jnp.float32) ** steps_of(streams_of[5], (LAT_TILES, LON_TILES, MAXB, OB), ((0, 4), (1, 8)), -0.2, 0.2)), 0.001953125, 0.00390625),
        "obs_rows": touch_ends(jax.random.randint(streams_of[6], (LAT_TILES, LON_TILES, MAXB), 0, TLAT), jax.random.fold_in(streams_of[6], 1), 0, TLAT - 1).astype(jnp.int32),
        "obs_count": draw_obs_count(jax.random.fold_in(streams_of[9], 71), 0),
        "local_mask": touch_ends((jax.random.randint(streams_of[8], (LAT_TILES, LON_TILES, TLAT, 9), 0, 4) < 3).astype(jnp.int32), jax.random.fold_in(streams_of[8], 1), 0, 1),
    }


HIGHEST_PRECISION = lax.Precision.HIGHEST

def stencil_matrix(weights, starts, width):
    columns = jnp.arange(width, dtype=jnp.int32)
    dense = jnp.zeros(starts.shape + (width,), jnp.float32)
    for offset in range(weights.shape[1]):
        hit = starts[:, :, None] + offset == columns[None, None, :]
        dense = dense + jnp.where(hit, weights[:, offset, :, None].astype(jnp.float32), jnp.float32(0.0))
    return dense

def tile_partial(tile_state, interp, starts, levels, values, weights, block_rows, live_count):
    picked = jnp.take(tile_state, block_rows, axis=2).astype(jnp.float32)
    dense = stencil_matrix(interp, starts, tile_state.shape[3])
    projected = jnp.einsum('kfjc,joc->kfjo', picked, dense, precision=HIGHEST_PRECISION)
    obs_ens = lax.optimization_barrier(jnp.sum(projected * jnp.transpose(levels.astype(jnp.float32), (1, 0, 2))[None], axis=1))
    obs_mean = lax.optimization_barrier(jnp.mean(obs_ens, axis=0))
    obs_dev = obs_ens - obs_mean
    innov = values - obs_mean
    is_live = jnp.arange(values.shape[0], dtype=jnp.int32)[:, None] < live_count
    live = jnp.where(is_live, weights, jnp.zeros_like(weights))
    members = obs_dev.shape[0]
    flat_dev = obs_dev.reshape(members, -1)
    paired = jnp.concatenate([flat_dev.T, innov.reshape(-1, 1)], axis=1)
    return jnp.dot(flat_dev * live.reshape(1, -1), paired, precision=HIGHEST_PRECISION)

def ensemble_transform(summed, members):
    identity = jnp.eye(members, dtype=jnp.float32)
    system = (members - 1) * identity + summed[:, :, :members]
    target = summed[:, :, members]
    scale = jnp.sqrt(lax.optimization_barrier(jnp.sum(system * system, axis=(1, 2))))
    root_term = system / scale[:, None, None]
    inverse = jnp.broadcast_to(identity, system.shape)
    for repeat in range(NS_ITERS):
        middle = 1.5 * identity - 0.5 * jnp.einsum('bij,bjk->bik', inverse, root_term, precision=HIGHEST_PRECISION)
        root_term = jnp.einsum('bij,bjk->bik', root_term, middle, precision=HIGHEST_PRECISION)
        inverse = jnp.einsum('bij,bjk->bik', middle, inverse, precision=HIGHEST_PRECISION)
    half_step = jnp.einsum('bij,bj->bi', inverse, target, precision=HIGHEST_PRECISION)
    shift_mean = jnp.einsum('bij,bj->bi', inverse, half_step, precision=HIGHEST_PRECISION) / scale[:, None]
    spread = jnp.sqrt(jnp.float32(members - 1)) * inverse / jnp.sqrt(scale)[:, None, None]
    return (spread + shift_mean[:, :, None]).astype(jnp.bfloat16)

def reference(ensemble, obs_interp, obs_start, obs_levels, obs_values, obs_weight, obs_rows, obs_count, local_mask):
    members = K
    fields = NF
    grid = ensemble.reshape(members, fields, TLAT * LAT_TILES, TLON * LON_TILES)
    tile_total = LAT_TILES * LON_TILES

    def tile_slice(tile_index):
        lat_index = (tile_index // LON_TILES).astype(jnp.int32)
        lon_index = (tile_index % LON_TILES).astype(jnp.int32)
        anchor = jnp.int32(0)
        block = lax.dynamic_slice(grid, (anchor, anchor, lat_index * TLAT, lon_index * TLON), (members, fields, TLAT, TLON))
        return (block, lat_index, lon_index)

    def one_partial(tile_index):
        block, lat_index, lon_index = tile_slice(tile_index)
        return tile_partial(block, obs_interp[lat_index, lon_index], obs_start[lat_index, lon_index], obs_levels[lat_index, lon_index], obs_values[lat_index, lon_index], obs_weight[lat_index, lon_index], obs_rows[lat_index, lon_index], obs_count[lat_index, lon_index])
    tile_ids = jnp.arange(tile_total, dtype=jnp.int32)
    partials = lax.map(one_partial, tile_ids).reshape(LAT_TILES, LON_TILES, members, members + 1)
    lon_stack = jnp.stack([jnp.roll(partials, 1, axis=1), partials, jnp.roll(partials, -1, axis=1)], axis=2)
    zero_row = jnp.zeros_like(lon_stack[:1])
    north_rows = jnp.concatenate([zero_row, lon_stack[:-1]], axis=0)
    south_rows = jnp.concatenate([lon_stack[1:], zero_row], axis=0)
    partner = ((jnp.arange(LON_TILES, dtype=jnp.int32) + LON_TILES // 2) % LON_TILES).astype(jnp.int32)
    north_pole = lon_stack[0][partner][:, ::-1]
    north_rows = north_rows.at[0].set(north_pole)
    slot_sums = jnp.stack([north_rows, lon_stack, south_rows], axis=2).reshape(LAT_TILES, LON_TILES, 9, members * (members + 1))

    def one_tile(tile_index):
        block, lat_index, lon_index = tile_slice(tile_index)
        slot_mask = local_mask[lat_index, lon_index].astype(jnp.float32)
        summed = jnp.dot(slot_mask, slot_sums[lat_index, lon_index], precision=HIGHEST_PRECISION).reshape(TLAT, members, members + 1)
        transform = ensemble_transform(summed, members)
        ens_mean = lax.optimization_barrier(jnp.sum(block.astype(jnp.float32), axis=0)) / members
        deviation = (block.astype(jnp.float32) - ens_mean).astype(jnp.bfloat16)
        deviation = lax.optimization_barrier(deviation)
        transform = lax.optimization_barrier(transform)
        update = jnp.einsum('kfbc,bkl->lfbc', deviation.astype(jnp.float32), transform.astype(jnp.float32), precision=HIGHEST_PRECISION)
        return (ens_mean[None] + update).astype(jnp.bfloat16)
    blocks = lax.map(one_tile, tile_ids).reshape(LAT_TILES, LON_TILES, members, fields, TLAT, TLON)
    return jnp.transpose(blocks, (2, 3, 0, 4, 1, 5)).reshape(members, fields, TLAT * LAT_TILES, TLON * LON_TILES)
```

```python
import functools
import math

import jax
import jax.numpy as jnp
from jax import lax
from jax.experimental import pallas as pl
from jax.experimental.pallas import tpu as pltpu
from jax.sharding import PartitionSpec as P

NS_ITERS = 6
MESH = pl.DeviceIdType.MESH


def flip(index, by, size):
    total, bit = 0, 1
    while bit < size:
        total += lax.rem(lax.div(index, bit) + lax.div(by, bit), 2) * bit
        bit *= 2
    return total


def gather_kernel(
    plan,
    ens_ref,
    interp_in,
    starts_in,
    levels_in,
    values_in,
    weights_in,
    rows_ref,
    count_ref,
    state_out,
    slots_out,
    state_ref,
    interp_ref,
    starts_ref,
    levels_ref,
    values_ref,
    weights_ref,
    dense,
    by_row,
    wide,
    obs,
    partial,
    nothing,
    send_sem,
    recv_sem,
    slot_send,
    slot_recv,
    load_sem,
    hand_sem,
):
    lat_n, lon_n, share, tile_rows, tile_cols, levels_n, members, group = plan
    total = lat_n * lon_n
    packs = lon_n // group
    group_rows = group * share
    group_members = group_rows // levels_n
    slots_n, stencil = interp_ref.shape[2:4]
    lat, lon = lax.axis_index("lat"), lax.axis_index("lon")
    me = lat * lon_n + lon
    pack, place = lax.div(lon, group), lax.rem(lon, group)

    barrier = pltpu.get_barrier_semaphore()

    @pl.loop(1, total)
    def _(step):
        peer = lax.rem(me + step, total)
        pl.semaphore_signal(
            barrier,
            inc=1,
            device_id={"lat": peer // lon_n, "lon": lax.rem(peer, lon_n)},
            device_id_type=MESH,
        )

    pl.semaphore_wait(barrier, total - 1)

    def tile_copy(to_lat, to_lon, source):
        return pltpu.make_async_remote_copy(
            src_ref=ens_ref.at[
                :,
                pl.ds(pl.multiple_of(to_lat * tile_rows, tile_rows), tile_rows),
                pl.ds(pl.multiple_of(to_lon * tile_cols, tile_cols), tile_cols),
            ],
            dst_ref=state_ref.at[pl.ds(source * share, share)],
            send_sem=send_sem.at[to_lat * lon_n + to_lon],
            recv_sem=recv_sem.at[source],
            device_id={"lat": to_lat, "lon": to_lon},
            device_id_type=MESH,
        )

    def turns(g, step):
        back = lat_n - 1 - step
        near = (step if g == 0 else back, g)
        return near, (back, packs // 2 + g)

    own = pltpu.make_async_copy(
        ens_ref.at[
            :,
            pl.ds(pl.multiple_of(lat * tile_rows, tile_rows), tile_rows),
            pl.ds(pl.multiple_of(lon * tile_cols, tile_cols), tile_cols),
        ],
        state_ref.at[pl.ds(me * share, share)],
        recv_sem.at[me],
    )
    own.start()

    for g in range(packs // 2):

        @pl.loop(0, lat_n)
        def _(step):
            near, far = turns(g, step)

            @pl.loop(0, group)
            def _(i):
                for by_lat, by_pack in (far, near):
                    to_lat = flip(lat, by_lat, lat_n)
                    to_lon = flip(pack, by_pack, packs) * group + lax.rem(place + i, group)

                    @pl.when(to_lat * lon_n + to_lon != me)
                    def _():
                        tile_copy(to_lat, to_lon, me).start()

    loads = [
        pltpu.make_async_copy(source, target, load_sem.at[i])
        for i, (source, target) in enumerate(
            [
                (interp_in, interp_ref),
                (starts_in, starts_ref),
                (levels_in, levels_ref),
                (values_in, values_ref),
                (weights_in, weights_ref),
            ]
        )
    ]
    for copy in loads:
        copy.start()
    for copy in loads:
        copy.wait()

    cells = lax.broadcasted_iota(jnp.int32, (tile_cols, starts_ref.shape[-1]), 0)

    @pl.loop(0, slots_n)
    def _(j):
        first = starts_ref[0, 0, pl.ds(j, 1), :]
        taps = interp_ref[0, 0, j].astype(jnp.float32)
        offset = cells - first
        grid = jnp.zeros(cells.shape, jnp.float32)
        for p in range(stencil):
            grid = jnp.where(offset == p, taps[p : p + 1, :], grid)
        dense[j] = grid.astype(jnp.bfloat16)

    def hand_on(which):
        piece = pl.ds(which * group_rows, group_rows)
        return pltpu.make_async_copy(state_ref.at[piece], state_out.at[piece], hand_sem.at[which])

    def take_group(which):
        base = which * group_rows

        @pl.loop(0, group)
        def _(i):
            source = which * group + i
            tile_copy(source // lon_n, lax.rem(source, lon_n), source).wait_recv()

        hand_on(which).start()

        @pl.loop(0, group_members)
        def _(i):
            piece = state_ref[pl.ds(base + i * levels_n, levels_n)].astype(jnp.float32)
            span = levels_n * tile_rows
            wide[pl.ds(pl.multiple_of(i * span, span), span), :] = piece.reshape(span, tile_cols)

        for r in range(tile_rows):
            by_row[r] = wide[pl.ds(r, group_rows, stride=tile_rows), :].astype(jnp.bfloat16)

        first = which * group_members * slots_n

        @pl.loop(0, slots_n, unroll=4)
        def _(j):
            product = jnp.dot(by_row[rows_ref[j]], dense[j], preferred_element_type=jnp.float32)
            level = levels_ref[0, 0, j].astype(jnp.float32)
            obs[pl.ds(first + j, group_members, stride=slots_n), :] = jnp.sum(
                product.reshape(group_members, levels_n, product.shape[1]) * level[None], axis=1
            )

    for g in range(packs // 2):

        @pl.loop(0, lat_n)
        def _(step):
            for by_lat, by_pack in turns(g, step):
                take_group(flip(lat, by_lat, lat_n) * packs + flip(pack, by_pack, packs))

    span, width = partial.shape
    blank = jnp.zeros((width - members, tile_cols), jnp.float32)

    def add_blocks(pair, carry):
        lefts, rights = [], []
        for i in range(2):
            j = pair * 2 + i
            block = obs[pl.ds(j, members, stride=slots_n), :]
            mean = jnp.sum(block, axis=0, keepdims=True) / members
            dev = block - mean
            innov = values_ref[0, 0, pl.ds(j, 1), :] - mean
            weight = weights_ref[0, 0, pl.ds(j, 1), :]
            live = jnp.where(jnp.full(weight.shape, j, jnp.int32) < count_ref[0], weight, 0.0)
            tail = jnp.broadcast_to(innov, (span - members, tile_cols))
            lefts.append(jnp.concatenate([dev, tail], axis=0).astype(jnp.bfloat16))
            rights.append(jnp.concatenate([dev * live, blank], axis=0).astype(jnp.bfloat16))
        return carry + lax.dot_general(
            jnp.concatenate(lefts, axis=1),
            jnp.concatenate(rights, axis=1),
            (((1,), (1,)), ((), ())),
            preferred_element_type=jnp.float32,
        )

    partial[...] = lax.fori_loop(
        0, slots_n // 2, add_blocks, jnp.zeros((span, width), jnp.float32), unroll=4
    )

    def slot_copy(to_lat, to_lon, slot, out):
        return pltpu.make_async_remote_copy(
            src_ref=partial,
            dst_ref=slots_out.at[slot],
            send_sem=slot_send.at[out],
            recv_sem=slot_recv.at[slot],
            device_id={"lat": to_lat, "lon": to_lon},
            device_id_type=MESH,
        )

    def away(distance):
        return lax.rem(lon + lon_n + distance, lon_n)

    last = lat_n - 1
    east_west = [slot_copy(lat, away(1), 3, 3), slot_copy(lat, away(-1), 5, 5)]
    south = [slot_copy(lat + 1, away(1 - s), s, s) for s in range(3)]
    north = [slot_copy(lat - 1, away(1 - s), 6 + s, 6 + s) for s in range(3)]
    pole = [slot_copy(lat, away(s - 1 - lon_n // 2), s, 6 + s) for s in range(3)]
    middle = pltpu.make_async_copy(partial, slots_out.at[4], slot_recv.at[4])
    outside = [
        pltpu.make_async_copy(nothing, slots_out.at[6 + s], slot_recv.at[6 + s]) for s in range(3)
    ]

    @pl.when(lat == 0)
    def _():
        for copy in pole:
            copy.start()

    for copy in east_west:
        copy.start()

    @pl.when(lat < last)
    def _():
        for copy in south:
            copy.start()

    @pl.when(lat > 0)
    def _():
        for copy in north:
            copy.start()

    middle.start()

    @pl.when(lat == last)
    def _():
        nothing[...] = jnp.zeros_like(nothing)
        for copy in outside:
            copy.start()

    @pl.loop(0, total)
    def _(peer):
        @pl.when(peer != me)
        def _():
            tile_copy(peer // lon_n, lax.rem(peer, lon_n), me).wait_send()

    @pl.loop(0, total // group)
    def _(which):
        hand_on(which).wait()

    middle.wait()
    for copy in east_west:
        copy.wait()
    for copy in pole:
        copy.wait_recv()
        copy.wait_send()

    @pl.when(lat < last)
    def _():
        for copy in south:
            copy.wait_send()
        for copy in north:
            copy.wait_recv()

    @pl.when(lat == last)
    def _():
        for copy in outside:
            copy.wait()


def halves(x):
    high = x.astype(jnp.bfloat16)
    return high, (x - high.astype(jnp.float32)).astype(jnp.bfloat16)


def split_dot(left, right):
    left_high, left_low = left
    right_high, right_low = right
    members, width = right_high.shape
    blank = jnp.zeros((width - members, 2 * width), jnp.bfloat16)
    top = jnp.concatenate([right_high, right_low], axis=1)
    low = jnp.concatenate([right_high, jnp.zeros_like(right_low)], axis=1)
    out = jnp.dot(
        jnp.concatenate([left_high, left_low], axis=1),
        jnp.concatenate([top, blank, low, blank], axis=0),
        preferred_element_type=jnp.float32,
    )
    return out[:, :width] + out[:, width:]


def analysis_kernel(
    plan,
    state_in,
    slots_in,
    mask_in,
    out_ref,
    state,
    slots,
    mask,
    chosen,
    root,
    inverse,
    scales,
    target,
    stack,
    spots,
    big,
    dev,
    mean,
    result,
    state_sem,
    slot_sem,
    mask_sem,
    out_sem,
):
    members, levels_n, tile_rows, tile_cols, ns_iters = plan
    width = slots.shape[2]
    deep = members * tile_rows
    parts = ns_iters - 2
    per = levels_n // parts
    tiles = range(tile_rows)

    load_mask = pltpu.make_async_copy(mask_in, mask, mask_sem)
    load_mask.start()
    load_slots = pltpu.make_async_copy(slots_in, slots, slot_sem)
    load_slots.start()

    def load_state(i):
        piece = pl.ds(i * per, per)
        return pltpu.make_async_copy(state_in.at[:, piece], state.at[:, piece], state_sem.at[i])

    for i in range(parts):
        load_state(i).start()

    rows = lax.broadcasted_iota(jnp.int32, (members, width), 0)
    cols = lax.broadcasted_iota(jnp.int32, (members, width), 1)
    identity = jnp.where(rows == cols, 1.0, 0.0)
    source = lax.broadcasted_iota(jnp.int32, (width, deep), 0)
    spot = lax.broadcasted_iota(jnp.int32, (width, deep), 1) - source * tile_rows
    spots[...] = jnp.where((spot >= 0) & (spot < tile_rows), 1.0, 0.0).astype(jnp.bfloat16)

    load_mask.wait()
    use = mask[0, 0].astype(jnp.float32)
    for slot in range(9):
        chosen[slot] = jnp.broadcast_to(use[:, slot : slot + 1], chosen.shape[1:])

    load_slots.wait()

    systems, totals = [], []
    for b in tiles:
        summed = chosen[0, b : b + 1] * slots[0]
        for slot in range(1, 9):
            summed += chosen[slot, b : b + 1] * slots[slot]
        target[b] = summed[members:]
        system = (members - 1) * identity + summed[:members]
        totals.append(jnp.sum(system * system, axis=0, keepdims=True))
        systems.append(system)
    scale = jnp.sqrt(jnp.sum(jnp.concatenate(totals, axis=0), axis=1, keepdims=True))
    scales[...] = jnp.broadcast_to(scale, scales.shape)
    inverse_scale = 1.0 / scale
    roots = [systems[b] * inverse_scale[b : b + 1] for b in tiles]
    middles = [halves(1.5 * identity - 0.5 * roots[b]) for b in tiles]

    def put(ref, b, pair):
        ref[b, 0], ref[b, 1] = pair

    def get(ref, b):
        return ref[b, 0], ref[b, 1]

    for b in tiles:
        put(inverse, b, middles[b])
        put(root, b, halves(split_dot(halves(roots[b]), middles[b])))

    @pl.loop(0, parts)
    def _(repeat):
        products = [split_dot(get(inverse, b), get(root, b)) for b in tiles]
        load_state(repeat).wait()
        for i in range(per):
            f = repeat * per + i
            cell = state[:, f].astype(jnp.float32)
            average = jnp.sum(cell, axis=0) / members
            mean[f] = average
            dev[f] = (cell - average[None]).reshape(deep, tile_cols).astype(jnp.bfloat16)
        middles = [halves(1.5 * identity - 0.5 * product) for product in products]
        new_root = [split_dot(get(root, b), middles[b]) for b in tiles]
        new_inverse = [split_dot(middles[b], get(inverse, b)) for b in tiles]
        for b in tiles:
            put(root, b, halves(new_root[b]))
            put(inverse, b, halves(new_inverse[b]))

    products = [split_dot(get(inverse, b), get(root, b)) for b in tiles]
    middles = [halves(1.5 * identity - 0.5 * product) for product in products]
    terms = [split_dot(middles[b], get(inverse, b)) for b in tiles]
    scale = scales[...]
    root_scale = jnp.sqrt(jnp.float32(members - 1)) / jnp.sqrt(scale)
    inverse_scale = 1.0 / scale
    for b in tiles:
        half_step = jnp.sum(terms[b] * target[b][:1], axis=1, keepdims=True)
        shift = jnp.sum(terms[b] * half_step, axis=0, keepdims=True) * inverse_scale[b : b + 1]
        stack[pl.ds(b, members, stride=tile_rows), :] = terms[b] * root_scale[b : b + 1] + shift

    lane = lax.broadcasted_iota(jnp.int32, (tile_rows, tile_cols), 1)
    same = lax.rem(lane, tile_rows) == lax.broadcasted_iota(jnp.int32, lane.shape, 0)
    step = 128
    for first in range(0, deep, step):
        wide = jnp.dot(
            stack[first : first + step].astype(jnp.bfloat16),
            spots[...],
            preferred_element_type=jnp.float32,
        )
        for left in range(0, deep, tile_cols):
            block = wide[:, left : left + tile_cols].reshape(-1, tile_rows, tile_cols)
            big[first : first + step, left : left + tile_cols] = (
                jnp.where(same[None], block, 0.0).reshape(step, tile_cols).astype(jnp.bfloat16)
            )

    def send(pair):
        return pltpu.make_async_copy(
            result.at[:, pl.ds(pair * 2, 2)], out_ref.at[:, pl.ds(pair * 2, 2)], out_sem.at[pair]
        )

    @pl.loop(0, levels_n // 2)
    def _(pair):
        f = pair * 2
        right = jnp.concatenate([dev[f], dev[f + 1]], axis=1)
        update = jnp.dot(big[...], right, preferred_element_type=jnp.float32)
        for half in range(2):
            block = update[:, half * tile_cols : (half + 1) * tile_cols].reshape(
                members, tile_rows, tile_cols
            )
            result[:, f + half] = (block + mean[f + half][None]).astype(jnp.bfloat16)
        send(pair).start()

    @pl.loop(0, levels_n // 2)
    def _(pair):
        send(pair).wait()


def per_device(
    ensemble,
    obs_interp,
    obs_start,
    obs_levels,
    obs_values,
    obs_weight,
    obs_rows,
    obs_count,
    local_mask,
):
    lat_n = lax.axis_size("lat")
    lon_n = lax.axis_size("lon")
    total = lat_n * lon_n
    share, grid_rows, grid_cols = ensemble.shape
    tile_rows = grid_rows // lat_n
    tile_cols = grid_cols // lon_n
    slots_n, levels_n, obs_n = obs_levels.shape[2:]
    members = share * total // levels_n
    group = math.lcm(share, levels_n) // share
    groups = total // group
    span, width = members + 8, -(-members // 128) * 128
    plan = (lat_n, lon_n, share, tile_rows, tile_cols, levels_n, members, group)
    hbm = pl.BlockSpec(memory_space=pltpu.HBM)
    smem = pl.BlockSpec(memory_space=pltpu.SMEM)
    state, slots = pl.pallas_call(
        functools.partial(gather_kernel, plan),
        out_shape=(
            jax.ShapeDtypeStruct((share * total, tile_rows, tile_cols), jnp.bfloat16),
            jax.ShapeDtypeStruct((9, span, width), jnp.float32),
        ),
        in_specs=[hbm] * 6 + [smem] * 2,
        out_specs=(hbm, hbm),
        scratch_shapes=[pltpu.VMEM((share * total, tile_rows, tile_cols), jnp.bfloat16)]
        + [
            pltpu.VMEM(array.shape, array.dtype)
            for array in (obs_interp, obs_start, obs_levels, obs_values, obs_weight)
        ]
        + [
            pltpu.VMEM((slots_n, tile_cols, obs_n), jnp.bfloat16),
            pltpu.VMEM((tile_rows, group * share, tile_cols), jnp.bfloat16),
            pltpu.VMEM((group * share * tile_rows, tile_cols), jnp.float32),
            pltpu.VMEM((members * slots_n, obs_n), jnp.float32),
            pltpu.VMEM((span, width), jnp.float32),
            pltpu.VMEM((span, width), jnp.float32),
            pltpu.SemaphoreType.DMA((total,)),
            pltpu.SemaphoreType.DMA((total,)),
            pltpu.SemaphoreType.DMA((9,)),
            pltpu.SemaphoreType.DMA((9,)),
            pltpu.SemaphoreType.DMA((5,)),
            pltpu.SemaphoreType.DMA((groups,)),
        ],
        compiler_params=pltpu.CompilerParams(
            collective_id=0, has_side_effects=True, vmem_limit_bytes=60 * 1024 * 1024
        ),
    )(
        ensemble,
        obs_interp,
        obs_start,
        obs_levels,
        obs_values,
        obs_weight,
        obs_rows.reshape(-1),
        obs_count.reshape(-1),
    )
    tile_state = state.reshape(members, levels_n, tile_rows, tile_cols)
    deep = members * tile_rows
    pairs = (tile_rows, 2, members, width)
    return pl.pallas_call(
        functools.partial(
            analysis_kernel, (members, levels_n, tile_rows, tile_cols, NS_ITERS)
        ),
        out_shape=jax.ShapeDtypeStruct(tile_state.shape, jnp.bfloat16),
        in_specs=[hbm, hbm, hbm],
        out_specs=hbm,
        scratch_shapes=[
            pltpu.VMEM(tile_state.shape, jnp.bfloat16),
            pltpu.VMEM(slots.shape, jnp.float32),
            pltpu.VMEM(local_mask.shape, jnp.int32),
            pltpu.VMEM((9, tile_rows, width), jnp.float32),
            pltpu.VMEM(pairs, jnp.bfloat16),
            pltpu.VMEM(pairs, jnp.bfloat16),
            pltpu.VMEM((tile_rows, width), jnp.float32),
            pltpu.VMEM((tile_rows, span - members, width), jnp.float32),
            pltpu.VMEM((deep, width), jnp.float32),
            pltpu.VMEM((width, deep), jnp.bfloat16),
            pltpu.VMEM((deep, deep), jnp.bfloat16),
            pltpu.VMEM((levels_n, deep, tile_cols), jnp.bfloat16),
            pltpu.VMEM((levels_n, tile_rows, tile_cols), jnp.float32),
            pltpu.VMEM(tile_state.shape, jnp.bfloat16),
            pltpu.SemaphoreType.DMA((NS_ITERS - 2,)),
            pltpu.SemaphoreType.DMA,
            pltpu.SemaphoreType.DMA,
            pltpu.SemaphoreType.DMA((levels_n // 2,)),
        ],
        compiler_params=pltpu.CompilerParams(vmem_limit_bytes=60 * 1024 * 1024),
    )(tile_state, slots, local_mask)


def solution(mesh):
    placed = (
        P(("lat", "lon"), None, None),
        P("lat", "lon", None, None, None),
        P("lat", "lon", None, None),
        P("lat", "lon", None, None, None),
        P("lat", "lon", None, None),
        P("lat", "lon", None, None),
        P("lat", "lon", None),
        P("lat", "lon"),
        P("lat", "lon", None, None),
    )
    return jax.shard_map(
        per_device,
        mesh=mesh,
        in_specs=placed,
        out_specs=P(None, None, "lat", "lon"),
        check_vma=False,
    )
```

```python
import functools
import math

import jax
import jax.numpy as jnp
from jax import lax
from jax.experimental import pallas as pl
from jax.experimental.pallas import tpu as pltpu
from jax.sharding import PartitionSpec as P

NS_ITERS = 6
MESH = pl.DeviceIdType.MESH


def flip(index, by, size):
    total, bit = 0, 1
    while bit < size:
        total += lax.rem(lax.div(index, bit) + lax.div(by, bit), 2) * bit
        bit *= 2
    return total


def gather_kernel(
    plan,
    ens_ref,
    interp_in,
    starts_in,
    levels_in,
    values_in,
    weights_in,
    rows_ref,
    count_ref,
    state_out,
    slots_out,
    state_ref,
    interp_ref,
    starts_ref,
    levels_ref,
    values_ref,
    weights_ref,
    dense,
    by_row,
    wide,
    obs,
    partial,
    nothing,
    send_sem,
    recv_sem,
    slot_send,
    slot_recv,
    load_sem,
    hand_sem,
):
    lat_n, lon_n, share, tile_rows, tile_cols, levels_n, members, group = plan
    total = lat_n * lon_n
    packs = lon_n // group
    group_rows = group * share
    group_members = group_rows // levels_n
    slots_n, stencil = interp_ref.shape[2:4]
    lat, lon = lax.axis_index("lat"), lax.axis_index("lon")
    me = lat * lon_n + lon
    pack, place = lax.div(lon, group), lax.rem(lon, group)

    barrier = pltpu.get_barrier_semaphore()

    @pl.loop(1, total)
    def _(step):
        peer = lax.rem(me + step, total)
        pl.semaphore_signal(
            barrier,
            inc=1,
            device_id={"lat": peer // lon_n, "lon": lax.rem(peer, lon_n)},
            device_id_type=MESH,
        )

    pl.semaphore_wait(barrier, total - 1)

    def tile_copy(to_lat, to_lon, source):
        return pltpu.make_async_remote_copy(
            src_ref=ens_ref.at[
                :,
                pl.ds(pl.multiple_of(to_lat * tile_rows, tile_rows), tile_rows),
                pl.ds(pl.multiple_of(to_lon * tile_cols, tile_cols), tile_cols),
            ],
            dst_ref=state_ref.at[pl.ds(source * share, share)],
            send_sem=send_sem.at[to_lat * lon_n + to_lon],
            recv_sem=recv_sem.at[source],
            device_id={"lat": to_lat, "lon": to_lon},
            device_id_type=MESH,
        )

    def turn(t):
        far, step, g = lax.rem(t, 2), lax.rem(lax.div(t, 2), lat_n), lax.div(t, 2 * lat_n)
        back = lat_n - 1 - step
        turned = lax.div(g + packs - 1, packs) * (1 - far) + far
        by_lat = turned * back + (1 - turned) * step
        by_pack = far * (packs // 2) + g
        return flip(lat, by_lat, lat_n), flip(pack, by_pack, packs)

    own = pltpu.make_async_copy(
        ens_ref.at[
            :,
            pl.ds(pl.multiple_of(lat * tile_rows, tile_rows), tile_rows),
            pl.ds(pl.multiple_of(lon * tile_cols, tile_cols), tile_cols),
        ],
        state_ref.at[pl.ds(me * share, share)],
        recv_sem.at[me],
    )
    own.start()

    @pl.loop(0, lat_n * packs // 2)
    def _(step):
        @pl.loop(0, group)
        def _(i):
            for t in (step * 2 + 1, step * 2):
                to_lat, to_pack = turn(t)
                to_lon = to_pack * group + lax.rem(place + i, group)

                @pl.when(to_lat * lon_n + to_lon != me)
                def _():
                    tile_copy(to_lat, to_lon, me).start()

    loads = [
        pltpu.make_async_copy(source, target, load_sem.at[i])
        for i, (source, target) in enumerate(
            [
                (interp_in, interp_ref),
                (starts_in, starts_ref),
                (levels_in, levels_ref),
                (values_in, values_ref),
                (weights_in, weights_ref),
            ]
        )
    ]
    for copy in loads:
        copy.start()
    for copy in loads:
        copy.wait()

    cells = lax.broadcasted_iota(jnp.int32, (tile_cols, starts_ref.shape[-1]), 0)

    @pl.loop(0, slots_n, unroll=4)
    def _(j):
        first = starts_ref[0, 0, pl.ds(j, 1), :]
        taps = interp_ref[0, 0, j].astype(jnp.float32)
        offset = cells - first
        grid = jnp.zeros(cells.shape, jnp.float32)
        for p in range(stencil):
            grid = jnp.where(offset == p, taps[p : p + 1, :], grid)
        dense[j] = grid.astype(jnp.bfloat16)

    def hand_on(which):
        piece = pl.ds(which * group_rows, group_rows)
        return pltpu.make_async_copy(state_ref.at[piece], state_out.at[piece], hand_sem.at[which])

    def take_group(which):
        base = which * group_rows

        @pl.loop(0, group)
        def _(i):
            source = which * group + i
            tile_copy(source // lon_n, lax.rem(source, lon_n), source).wait_recv()

        hand_on(which).start()

        @pl.loop(0, group_members)
        def _(i):
            piece = state_ref[pl.ds(base + i * levels_n, levels_n)].astype(jnp.float32)
            span = levels_n * tile_rows
            wide[pl.ds(pl.multiple_of(i * span, span), span), :] = piece.reshape(span, tile_cols)

        for r in range(tile_rows):
            by_row[r] = wide[pl.ds(r, group_rows, stride=tile_rows), :].astype(jnp.bfloat16)

        first = which * group_members * slots_n

        @pl.loop(0, slots_n, unroll=slots_n)
        def _(j):
            product = jnp.dot(by_row[rows_ref[j]], dense[j], preferred_element_type=jnp.float32)
            level = levels_ref[0, 0, j].astype(jnp.float32)
            obs[pl.ds(first + j, group_members, stride=slots_n), :] = jnp.sum(
                product.reshape(group_members, levels_n, product.shape[1]) * level[None], axis=1
            )

    @pl.loop(0, lat_n * packs)
    def _(t):
        from_lat, from_pack = turn(t)
        take_group(from_lat * packs + from_pack)

    span, width = partial.shape
    blank = jnp.zeros((width - members, tile_cols), jnp.float32)

    def add_blocks(pair, carry):
        lefts, rights = [], []
        for i in range(2):
            j = pair * 2 + i
            block = obs[pl.ds(j, members, stride=slots_n), :]
            mean = jnp.sum(block, axis=0, keepdims=True) / members
            dev = block - mean
            innov = values_ref[0, 0, pl.ds(j, 1), :] - mean
            weight = weights_ref[0, 0, pl.ds(j, 1), :]
            live = jnp.where(jnp.full(weight.shape, j, jnp.int32) < count_ref[0], weight, 0.0)
            tail = jnp.broadcast_to(innov, (span - members, tile_cols))
            lefts.append(jnp.concatenate([dev, tail], axis=0).astype(jnp.bfloat16))
            rights.append(jnp.concatenate([dev * live, blank], axis=0).astype(jnp.bfloat16))
        return carry + lax.dot_general(
            jnp.concatenate(lefts, axis=1),
            jnp.concatenate(rights, axis=1),
            (((1,), (1,)), ((), ())),
            preferred_element_type=jnp.float32,
        )

    partial[...] = lax.fori_loop(
        0, slots_n // 2, add_blocks, jnp.zeros((span, width), jnp.float32), unroll=slots_n // 2
    )

    def slot_copy(to_lat, to_lon, slot, out):
        return pltpu.make_async_remote_copy(
            src_ref=partial,
            dst_ref=slots_out.at[slot],
            send_sem=slot_send.at[out],
            recv_sem=slot_recv.at[slot],
            device_id={"lat": to_lat, "lon": to_lon},
            device_id_type=MESH,
        )

    def away(distance):
        return lax.rem(lon + lon_n + distance, lon_n)

    last = lat_n - 1
    east_west = [slot_copy(lat, away(1), 3, 3), slot_copy(lat, away(-1), 5, 5)]
    south = [slot_copy(lat + 1, away(1 - s), s, s) for s in range(3)]
    north = [slot_copy(lat - 1, away(1 - s), 6 + s, 6 + s) for s in range(3)]
    pole = [slot_copy(lat, away(s - 1 - lon_n // 2), s, 6 + s) for s in range(3)]
    middle = pltpu.make_async_copy(partial, slots_out.at[4], slot_recv.at[4])
    outside = [
        pltpu.make_async_copy(nothing, slots_out.at[6 + s], slot_recv.at[6 + s]) for s in range(3)
    ]

    @pl.when(lat == 0)
    def _():
        for copy in pole:
            copy.start()

    for copy in east_west:
        copy.start()

    @pl.when(lat < last)
    def _():
        for copy in south:
            copy.start()

    @pl.when(lat > 0)
    def _():
        for copy in north:
            copy.start()

    middle.start()

    @pl.when(lat == last)
    def _():
        nothing[...] = jnp.zeros_like(nothing)
        for copy in outside:
            copy.start()

    @pl.loop(0, total)
    def _(peer):
        @pl.when(peer != me)
        def _():
            tile_copy(peer // lon_n, lax.rem(peer, lon_n), me).wait_send()

    @pl.loop(0, total // group)
    def _(which):
        hand_on(which).wait()

    middle.wait()
    for copy in east_west:
        copy.wait()
    for copy in pole:
        copy.wait_recv()
        copy.wait_send()

    @pl.when(lat < last)
    def _():
        for copy in south:
            copy.wait_send()
        for copy in north:
            copy.wait_recv()

    @pl.when(lat == last)
    def _():
        for copy in outside:
            copy.wait()


def halves(x):
    high = x.astype(jnp.bfloat16)
    return high, (x - high.astype(jnp.float32)).astype(jnp.bfloat16)


def split_dot(left, right):
    left_high, left_low = left
    right_high, right_low = right
    members, width = right_high.shape
    blank = jnp.zeros((width - members, 2 * width), jnp.bfloat16)
    top = jnp.concatenate([right_high, right_low], axis=1)
    low = jnp.concatenate([right_high, jnp.zeros_like(right_low)], axis=1)
    out = jnp.dot(
        jnp.concatenate([left_high, left_low], axis=1),
        jnp.concatenate([top, blank, low, blank], axis=0),
        preferred_element_type=jnp.float32,
    )
    return out[:, :width] + out[:, width:]


def analysis_kernel(
    plan,
    state_in,
    slots_in,
    mask_in,
    out_ref,
    state,
    slots,
    mask,
    chosen,
    root,
    inverse,
    scales,
    target,
    stack,
    spots,
    big,
    dev,
    mean,
    result,
    state_sem,
    slot_sem,
    mask_sem,
    out_sem,
):
    members, levels_n, tile_rows, tile_cols, ns_iters = plan
    width = slots.shape[2]
    deep = members * tile_rows
    parts = ns_iters - 2
    per = levels_n // parts
    tiles = range(tile_rows)

    load_mask = pltpu.make_async_copy(mask_in, mask, mask_sem)
    load_mask.start()
    load_slots = pltpu.make_async_copy(slots_in, slots, slot_sem)
    load_slots.start()

    def load_state(i):
        piece = pl.ds(i * per, per)
        return pltpu.make_async_copy(state_in.at[:, piece], state.at[:, piece], state_sem.at[i])

    for i in range(parts):
        load_state(i).start()

    rows = lax.broadcasted_iota(jnp.int32, (members, width), 0)
    cols = lax.broadcasted_iota(jnp.int32, (members, width), 1)
    identity = jnp.where(rows == cols, 1.0, 0.0)
    source = lax.broadcasted_iota(jnp.int32, (width, deep), 0)
    spot = lax.broadcasted_iota(jnp.int32, (width, deep), 1) - source * tile_rows
    spots[...] = jnp.where((spot >= 0) & (spot < tile_rows), 1.0, 0.0).astype(jnp.bfloat16)

    load_mask.wait()
    use = mask[0, 0].astype(jnp.float32)
    for slot in range(9):
        chosen[slot] = jnp.broadcast_to(use[:, slot : slot + 1], chosen.shape[1:])

    load_slots.wait()

    systems, totals = [], []
    for b in tiles:
        summed = chosen[0, b : b + 1] * slots[0]
        for slot in range(1, 9):
            summed += chosen[slot, b : b + 1] * slots[slot]
        target[b] = summed[members:]
        system = (members - 1) * identity + summed[:members]
        totals.append(jnp.sum(system * system, axis=0, keepdims=True))
        systems.append(system)
    scale = jnp.sqrt(jnp.sum(jnp.concatenate(totals, axis=0), axis=1, keepdims=True))
    scales[...] = jnp.broadcast_to(scale, scales.shape)
    inverse_scale = 1.0 / scale
    roots = [systems[b] * inverse_scale[b : b + 1] for b in tiles]
    middles = [halves(1.5 * identity - 0.5 * roots[b]) for b in tiles]

    def put(ref, b, pair):
        ref[b, 0], ref[b, 1] = pair

    def get(ref, b):
        return ref[b, 0], ref[b, 1]

    for b in tiles:
        put(inverse, b, middles[b])
        put(root, b, halves(split_dot(halves(roots[b]), middles[b])))

    @pl.loop(0, parts)
    def _(repeat):
        products = [split_dot(get(inverse, b), get(root, b)) for b in tiles]
        load_state(repeat).wait()
        for i in range(per):
            f = repeat * per + i
            cell = state[:, f].astype(jnp.float32)
            average = jnp.sum(cell, axis=0) / members
            mean[f] = average
            dev[f] = (cell - average[None]).reshape(deep, tile_cols).astype(jnp.bfloat16)
        middles = [halves(1.5 * identity - 0.5 * product) for product in products]
        new_root = [split_dot(get(root, b), middles[b]) for b in tiles]
        new_inverse = [split_dot(middles[b], get(inverse, b)) for b in tiles]
        for b in tiles:
            put(root, b, halves(new_root[b]))
            put(inverse, b, halves(new_inverse[b]))

    products = [split_dot(get(inverse, b), get(root, b)) for b in tiles]
    middles = [halves(1.5 * identity - 0.5 * product) for product in products]
    terms = [split_dot(middles[b], get(inverse, b)) for b in tiles]
    scale = scales[...]
    root_scale = jnp.sqrt(jnp.float32(members - 1)) / jnp.sqrt(scale)
    inverse_scale = 1.0 / scale
    for b in tiles:
        half_step = jnp.sum(terms[b] * target[b][:1], axis=1, keepdims=True)
        shift = jnp.sum(terms[b] * half_step, axis=0, keepdims=True) * inverse_scale[b : b + 1]
        stack[pl.ds(b, members, stride=tile_rows), :] = terms[b] * root_scale[b : b + 1] + shift

    lane = lax.broadcasted_iota(jnp.int32, (tile_rows, tile_cols), 1)
    same = lax.rem(lane, tile_rows) == lax.broadcasted_iota(jnp.int32, lane.shape, 0)
    step = 128
    for first in range(0, deep, step):
        wide = jnp.dot(
            stack[first : first + step].astype(jnp.bfloat16),
            spots[...],
            preferred_element_type=jnp.float32,
        )
        for left in range(0, deep, tile_cols):
            block = wide[:, left : left + tile_cols].reshape(-1, tile_rows, tile_cols)
            big[first : first + step, left : left + tile_cols] = (
                jnp.where(same[None], block, 0.0).reshape(step, tile_cols).astype(jnp.bfloat16)
            )

    def send(pair):
        return pltpu.make_async_copy(
            result.at[:, pl.ds(pair * 2, 2)], out_ref.at[:, pl.ds(pair * 2, 2)], out_sem.at[pair]
        )

    @pl.loop(0, levels_n // 2, unroll=4)
    def _(pair):
        f = pair * 2
        right = jnp.concatenate([dev[f], dev[f + 1]], axis=1)
        update = jnp.dot(big[...], right, preferred_element_type=jnp.float32)
        for half in range(2):
            block = update[:, half * tile_cols : (half + 1) * tile_cols].reshape(
                members, tile_rows, tile_cols
            )
            result[:, f + half] = (block + mean[f + half][None]).astype(jnp.bfloat16)
        send(pair).start()

    @pl.loop(0, levels_n // 2)
    def _(pair):
        send(pair).wait()


def per_device(
    ensemble,
    obs_interp,
    obs_start,
    obs_levels,
    obs_values,
    obs_weight,
    obs_rows,
    obs_count,
    local_mask,
):
    lat_n = lax.axis_size("lat")
    lon_n = lax.axis_size("lon")
    total = lat_n * lon_n
    share, grid_rows, grid_cols = ensemble.shape
    tile_rows = grid_rows // lat_n
    tile_cols = grid_cols // lon_n
    slots_n, levels_n, obs_n = obs_levels.shape[2:]
    members = share * total // levels_n
    group = math.lcm(share, levels_n) // share
    groups = total // group
    span, width = members + 8, -(-members // 128) * 128
    plan = (lat_n, lon_n, share, tile_rows, tile_cols, levels_n, members, group)
    hbm = pl.BlockSpec(memory_space=pltpu.HBM)
    smem = pl.BlockSpec(memory_space=pltpu.SMEM)
    state, slots = pl.pallas_call(
        functools.partial(gather_kernel, plan),
        out_shape=(
            jax.ShapeDtypeStruct((share * total, tile_rows, tile_cols), jnp.bfloat16),
            jax.ShapeDtypeStruct((9, span, width), jnp.float32),
        ),
        in_specs=[hbm] * 6 + [smem] * 2,
        out_specs=(hbm, hbm),
        scratch_shapes=[pltpu.VMEM((share * total, tile_rows, tile_cols), jnp.bfloat16)]
        + [
            pltpu.VMEM(array.shape, array.dtype)
            for array in (obs_interp, obs_start, obs_levels, obs_values, obs_weight)
        ]
        + [
            pltpu.VMEM((slots_n, tile_cols, obs_n), jnp.bfloat16),
            pltpu.VMEM((tile_rows, group * share, tile_cols), jnp.bfloat16),
            pltpu.VMEM((group * share * tile_rows, tile_cols), jnp.float32),
            pltpu.VMEM((members * slots_n, obs_n), jnp.float32),
            pltpu.VMEM((span, width), jnp.float32),
            pltpu.VMEM((span, width), jnp.float32),
            pltpu.SemaphoreType.DMA((total,)),
            pltpu.SemaphoreType.DMA((total,)),
            pltpu.SemaphoreType.DMA((9,)),
            pltpu.SemaphoreType.DMA((9,)),
            pltpu.SemaphoreType.DMA((5,)),
            pltpu.SemaphoreType.DMA((groups,)),
        ],
        compiler_params=pltpu.CompilerParams(
            collective_id=0, has_side_effects=True, vmem_limit_bytes=60 * 1024 * 1024
        ),
    )(
        ensemble,
        obs_interp,
        obs_start,
        obs_levels,
        obs_values,
        obs_weight,
        obs_rows.reshape(-1),
        obs_count.reshape(-1),
    )
    tile_state = state.reshape(members, levels_n, tile_rows, tile_cols)
    deep = members * tile_rows
    pairs = (tile_rows, 2, members, width)
    return pl.pallas_call(
        functools.partial(
            analysis_kernel, (members, levels_n, tile_rows, tile_cols, NS_ITERS)
        ),
        out_shape=jax.ShapeDtypeStruct(tile_state.shape, jnp.bfloat16),
        in_specs=[hbm, hbm, hbm],
        out_specs=hbm,
        scratch_shapes=[
            pltpu.VMEM(tile_state.shape, jnp.bfloat16),
            pltpu.VMEM(slots.shape, jnp.float32),
            pltpu.VMEM(local_mask.shape, jnp.int32),
            pltpu.VMEM((9, tile_rows, width), jnp.float32),
            pltpu.VMEM(pairs, jnp.bfloat16),
            pltpu.VMEM(pairs, jnp.bfloat16),
            pltpu.VMEM((tile_rows, width), jnp.float32),
            pltpu.VMEM((tile_rows, span - members, width), jnp.float32),
            pltpu.VMEM((deep, width), jnp.float32),
            pltpu.VMEM((width, deep), jnp.bfloat16),
            pltpu.VMEM((deep, deep), jnp.bfloat16),
            pltpu.VMEM((levels_n, deep, tile_cols), jnp.bfloat16),
            pltpu.VMEM((levels_n, tile_rows, tile_cols), jnp.float32),
            pltpu.VMEM(tile_state.shape, jnp.bfloat16),
            pltpu.SemaphoreType.DMA((NS_ITERS - 2,)),
            pltpu.SemaphoreType.DMA,
            pltpu.SemaphoreType.DMA,
            pltpu.SemaphoreType.DMA((levels_n // 2,)),
        ],
        compiler_params=pltpu.CompilerParams(vmem_limit_bytes=60 * 1024 * 1024),
    )(tile_state, slots, local_mask)


def solution(mesh):
    placed = (
        P(("lat", "lon"), None, None),
        P("lat", "lon", None, None, None),
        P("lat", "lon", None, None),
        P("lat", "lon", None, None, None),
        P("lat", "lon", None, None),
        P("lat", "lon", None, None),
        P("lat", "lon", None),
        P("lat", "lon"),
        P("lat", "lon", None, None),
    )
    return jax.shard_map(
        per_device,
        mesh=mesh,
        in_specs=placed,
        out_specs=P(None, None, "lat", "lon"),
        check_vma=False,
    )
```

```python
import functools
import math

import jax
import jax.numpy as jnp
from jax import lax
from jax.experimental import pallas as pl
from jax.experimental.pallas import tpu as pltpu
from jax.sharding import PartitionSpec as P

NS_ITERS = 6
MESH = pl.DeviceIdType.MESH


def flip(index, by, size):
    total, bit = 0, 1
    while bit < size:
        total += lax.rem(lax.div(index, bit) + lax.div(by, bit), 2) * bit
        bit *= 2
    return total


def gather_kernel(
    plan,
    ens_ref,
    interp_in,
    starts_in,
    levels_in,
    values_in,
    weights_in,
    rows_ref,
    count_ref,
    state_out,
    slots_out,
    state_ref,
    interp_ref,
    starts_ref,
    levels_ref,
    values_ref,
    weights_ref,
    dense,
    by_row,
    wide,
    obs,
    near,
    nothing,
    send_sem,
    recv_sem,
    near_send,
    near_recv,
    slot_send,
    slot_recv,
    polar_send,
    polar_recv,
    load_sem,
    hand_sem,
):
    lat_n, lon_n, share, tile_rows, tile_cols, levels_n, members, group = plan
    total = lat_n * lon_n
    packs = lon_n // group
    group_rows = group * share
    group_members = group_rows // levels_n
    slots_n, stencil = interp_ref.shape[2:4]
    lat, lon = lax.axis_index("lat"), lax.axis_index("lon")
    me = lat * lon_n + lon
    pack, place = lax.div(lon, group), lax.rem(lon, group)

    barrier = pltpu.get_barrier_semaphore()

    @pl.loop(1, total)
    def _(step):
        peer = lax.rem(me + step, total)
        pl.semaphore_signal(
            barrier,
            inc=1,
            device_id={"lat": peer // lon_n, "lon": lax.rem(peer, lon_n)},
            device_id_type=MESH,
        )

    pl.semaphore_wait(barrier, total - 1)

    def tile_copy(to_lat, to_lon, source):
        return pltpu.make_async_remote_copy(
            src_ref=ens_ref.at[
                :,
                pl.ds(pl.multiple_of(to_lat * tile_rows, tile_rows), tile_rows),
                pl.ds(pl.multiple_of(to_lon * tile_cols, tile_cols), tile_cols),
            ],
            dst_ref=state_ref.at[pl.ds(source * share, share)],
            send_sem=send_sem.at[to_lat * lon_n + to_lon],
            recv_sem=recv_sem.at[source],
            device_id={"lat": to_lat, "lon": to_lon},
            device_id_type=MESH,
        )

    def turn(t):
        far, step, g = lax.rem(t, 2), lax.rem(lax.div(t, 2), lat_n), lax.div(t, 2 * lat_n)
        back = lat_n - 1 - step
        turned = lax.div(g + packs - 1, packs) * (1 - far) + far
        by_lat = turned * back + (1 - turned) * step
        by_pack = far * (packs // 2) + g
        return flip(lat, by_lat, lat_n), flip(pack, by_pack, packs)

    own = pltpu.make_async_copy(
        ens_ref.at[
            :,
            pl.ds(pl.multiple_of(lat * tile_rows, tile_rows), tile_rows),
            pl.ds(pl.multiple_of(lon * tile_cols, tile_cols), tile_cols),
        ],
        state_ref.at[pl.ds(me * share, share)],
        recv_sem.at[me],
    )
    own.start()

    @pl.loop(0, lat_n * packs // 2)
    def _(step):
        @pl.loop(0, group)
        def _(i):
            for t in (step * 2 + 1, step * 2):
                to_lat, to_pack = turn(t)
                to_lon = to_pack * group + lax.rem(place + i, group)

                @pl.when(to_lat * lon_n + to_lon != me)
                def _():
                    tile_copy(to_lat, to_lon, me).start()

    loads = [
        pltpu.make_async_copy(source, target, load_sem.at[i])
        for i, (source, target) in enumerate(
            [
                (interp_in, interp_ref),
                (starts_in, starts_ref),
                (levels_in, levels_ref),
                (values_in, values_ref),
                (weights_in, weights_ref),
            ]
        )
    ]
    for copy in loads:
        copy.start()
    for copy in loads:
        copy.wait()

    last = lat_n - 1
    outside = pltpu.make_async_copy(nothing, slots_out.at[pl.ds(6, 3)], load_sem.at[2])

    @pl.when(lat == last)
    def _():
        nothing[...] = jnp.zeros_like(nothing)
        outside.start()

    cells = lax.broadcasted_iota(jnp.int32, (tile_cols, starts_ref.shape[-1]), 0)

    @pl.loop(0, slots_n, unroll=4)
    def _(j):
        first = starts_ref[0, 0, pl.ds(j, 1), :]
        taps = interp_ref[0, 0, j].astype(jnp.float32)
        offset = cells - first
        grid = jnp.zeros(cells.shape, jnp.float32)
        for p in range(stencil):
            grid = jnp.where(offset == p, taps[p : p + 1, :], grid)
        dense[j] = grid.astype(jnp.bfloat16)

    def hand_on(which):
        piece = pl.ds(which * group_rows, group_rows)
        return pltpu.make_async_copy(state_ref.at[piece], state_out.at[piece], hand_sem.at[which])

    def take_group(which):
        base = which * group_rows

        @pl.loop(0, group)
        def _(i):
            source = which * group + i
            tile_copy(source // lon_n, lax.rem(source, lon_n), source).wait_recv()

        hand_on(which).start()

        @pl.loop(0, group_members)
        def _(i):
            piece = state_ref[pl.ds(base + i * levels_n, levels_n)].astype(jnp.float32)
            span = levels_n * tile_rows
            wide[pl.ds(pl.multiple_of(i * span, span), span), :] = piece.reshape(span, tile_cols)

        for r in range(tile_rows):
            by_row[r] = wide[pl.ds(r, group_rows, stride=tile_rows), :].astype(jnp.bfloat16)

        first = which * group_members * slots_n

        @pl.loop(0, slots_n, unroll=slots_n)
        def _(j):
            product = jnp.dot(by_row[rows_ref[j]], dense[j], preferred_element_type=jnp.float32)
            level = levels_ref[0, 0, j].astype(jnp.float32)
            obs[pl.ds(first + j, group_members, stride=slots_n), :] = jnp.sum(
                product.reshape(group_members, levels_n, product.shape[1]) * level[None], axis=1
            )

    @pl.loop(0, lat_n * packs)
    def _(t):
        from_lat, from_pack = turn(t)
        take_group(from_lat * packs + from_pack)

    span, width = near.shape[1:]
    half = members // 2
    blank = jnp.zeros((width - members - half, tile_cols), jnp.float32)

    def add_blocks(pair, carry):
        lefts, rights = [], []
        for i in range(2):
            j = pair * 2 + i
            block = obs[pl.ds(j, members, stride=slots_n), :]
            mean = jnp.sum(block, axis=0, keepdims=True) / members
            dev = block - mean
            innov = values_ref[0, 0, pl.ds(j, 1), :] - mean
            weight = weights_ref[0, 0, pl.ds(j, 1), :]
            live = jnp.where(jnp.full(weight.shape, j, jnp.int32) < count_ref[0], weight, 0.0)
            tail = jnp.broadcast_to(innov, (8, tile_cols))
            lefts.append(jnp.concatenate([dev, tail], axis=0).astype(jnp.bfloat16))
            heavy = dev * live
            rights.append(
                jnp.concatenate([heavy, heavy[half:], blank], axis=0).astype(jnp.bfloat16)
            )
        return carry + lax.dot_general(
            jnp.concatenate(lefts, axis=1),
            jnp.concatenate(rights, axis=1),
            (((1,), (1,)), ((), ())),
            preferred_element_type=jnp.float32,
        )

    summed = lax.fori_loop(
        0, slots_n // 2, add_blocks, jnp.zeros((members + 8, width), jnp.float32), unroll=slots_n // 2
    )
    lane = lax.broadcasted_iota(jnp.int32, (half, width), 1)
    near[1, :half] = jnp.where(lane < members, summed[:half], summed[half:members])
    near[1, half:] = summed[members:]

    def pass_on(source, target, sems, i, to_lat, to_lon):
        send, recv = sems
        return pltpu.make_async_remote_copy(
            src_ref=source,
            dst_ref=target,
            send_sem=send.at[i],
            recv_sem=recv.at[i],
            device_id={"lat": to_lat, "lon": to_lon},
            device_id_type=MESH,
        )

    east, west = lax.rem(lon + 1, lon_n), lax.rem(lon + lon_n - 1, lon_n)
    across = lax.rem(lon + lon_n // 2, lon_n)
    first, second = (near_send, near_recv), (slot_send, slot_recv)
    polar = (polar_send, polar_recv)
    row_mates = [
        pass_on(near.at[1], near.at[0], first, 0, lat, east),
        pass_on(near.at[1], near.at[2], first, 2, lat, west),
    ]
    over_pole = [
        pass_on(near.at[1], slots_out.at[s], polar, s, lat, lax.rem(across + lon_n + s - 1, lon_n))
        for s in range(3)
    ]
    south = pass_on(near, slots_out.at[pl.ds(0, 3)], second, 0, lat + 1, lon)
    north = pass_on(near, slots_out.at[pl.ds(6, 3)], second, 1, lat - 1, lon)
    keep_near = pltpu.make_async_copy(near, slots_out.at[pl.ds(3, 3)], load_sem.at[0])

    @pl.when(lat == 0)
    def _():
        for copy in over_pole:
            copy.start()

    for copy in row_mates:
        copy.start()

    for copy in row_mates:
        copy.wait_recv()

    @pl.when(lat < last)
    def _():
        south.start()

    @pl.when(lat > 0)
    def _():
        north.start()

    keep_near.start()

    @pl.loop(0, total)
    def _(peer):
        @pl.when(peer != me)
        def _():
            tile_copy(peer // lon_n, lax.rem(peer, lon_n), me).wait_send()

    @pl.loop(0, total // group)
    def _(which):
        hand_on(which).wait()

    for copy in row_mates:
        copy.wait_send()
    keep_near.wait()

    @pl.when(lat == 0)
    def _():
        for copy in over_pole:
            copy.wait()

    @pl.when(lat > 0)
    def _():
        south.wait_recv()
        north.wait_send()

    @pl.when(lat < last)
    def _():
        south.wait_send()
        north.wait_recv()

    @pl.when(lat == last)
    def _():
        outside.wait()


def halves(x):
    high = x.astype(jnp.bfloat16)
    return high, (x - high.astype(jnp.float32)).astype(jnp.bfloat16)


def split_dot(left, right):
    left_high, left_low = left
    right_high, right_low = right
    members, width = right_high.shape
    blank = jnp.zeros((width - members, 2 * width), jnp.bfloat16)
    top = jnp.concatenate([right_high, right_low], axis=1)
    low = jnp.concatenate([right_high, jnp.zeros_like(right_low)], axis=1)
    out = jnp.dot(
        jnp.concatenate([left_high, left_low], axis=1),
        jnp.concatenate([top, blank, low, blank], axis=0),
        preferred_element_type=jnp.float32,
    )
    return out[:, :width] + out[:, width:]


def analysis_kernel(
    plan,
    state_in,
    slots_in,
    mask_in,
    out_ref,
    state,
    slots,
    mask,
    chosen,
    root,
    inverse,
    scales,
    target,
    stack,
    spots,
    big,
    dev,
    mean,
    result,
    state_sem,
    slot_sem,
    mask_sem,
    out_sem,
):
    members, levels_n, tile_rows, tile_cols, ns_iters = plan
    width = slots.shape[2]
    deep = members * tile_rows
    parts = ns_iters - 2
    per = levels_n // parts
    tiles = range(tile_rows)

    load_mask = pltpu.make_async_copy(mask_in, mask, mask_sem)
    load_mask.start()
    load_slots = pltpu.make_async_copy(slots_in, slots, slot_sem)
    load_slots.start()

    def load_state(i):
        piece = pl.ds(i * per, per)
        return pltpu.make_async_copy(state_in.at[:, piece], state.at[:, piece], state_sem.at[i])

    for i in range(parts):
        load_state(i).start()

    rows = lax.broadcasted_iota(jnp.int32, (members, width), 0)
    cols = lax.broadcasted_iota(jnp.int32, (members, width), 1)
    identity = jnp.where(rows == cols, 1.0, 0.0)
    source = lax.broadcasted_iota(jnp.int32, (width, deep), 0)
    spot = lax.broadcasted_iota(jnp.int32, (width, deep), 1) - source * tile_rows
    spots[...] = jnp.where((spot >= 0) & (spot < tile_rows), 1.0, 0.0).astype(jnp.bfloat16)

    load_mask.wait()
    use = mask[0, 0].astype(jnp.float32)
    for slot in range(9):
        chosen[slot] = jnp.broadcast_to(use[:, slot : slot + 1], chosen.shape[1:])

    load_slots.wait()

    half = members // 2
    lane = cols[:half]
    real = cols < members
    empty = jnp.zeros((width - half, width), jnp.float32)
    systems, totals = [], []
    for b in tiles:
        summed = chosen[0, b : b + 1] * slots[0]
        for slot in range(1, 9):
            summed += chosen[slot, b : b + 1] * slots[slot]
        target[b] = summed[half:]
        top = summed[:half]
        turned = pltpu.roll(top, width - half, 1)
        across = jnp.concatenate([turned, empty], axis=0).T[:half]
        bottom = jnp.where(lane < half, across, turned)
        whole = jnp.where(real, jnp.concatenate([top, bottom], axis=0), 0.0)
        system = (members - 1) * identity + whole
        totals.append(jnp.sum(system * system, axis=0, keepdims=True))
        systems.append(system)
    scale = jnp.sqrt(jnp.sum(jnp.concatenate(totals, axis=0), axis=1, keepdims=True))
    scales[...] = jnp.broadcast_to(scale, scales.shape)
    inverse_scale = 1.0 / scale
    roots = [systems[b] * inverse_scale[b : b + 1] for b in tiles]
    middles = [halves(1.5 * identity - 0.5 * roots[b]) for b in tiles]

    def put(ref, b, pair):
        ref[b, 0], ref[b, 1] = pair

    def get(ref, b):
        return ref[b, 0], ref[b, 1]

    for b in tiles:
        put(inverse, b, middles[b])
        put(root, b, halves(split_dot(halves(roots[b]), middles[b])))

    @pl.loop(0, parts)
    def _(repeat):
        products = [split_dot(get(inverse, b), get(root, b)) for b in tiles]
        load_state(repeat).wait()
        for i in range(per):
            f = repeat * per + i
            cell = state[:, f].astype(jnp.float32)
            average = jnp.sum(cell, axis=0) / members
            mean[f] = average
            dev[f] = (cell - average[None]).reshape(deep, tile_cols).astype(jnp.bfloat16)
        middles = [halves(1.5 * identity - 0.5 * product) for product in products]
        new_root = [split_dot(get(root, b), middles[b]) for b in tiles]
        new_inverse = [split_dot(middles[b], get(inverse, b)) for b in tiles]
        for b in tiles:
            put(root, b, halves(new_root[b]))
            put(inverse, b, halves(new_inverse[b]))

    products = [split_dot(get(inverse, b), get(root, b)) for b in tiles]
    middles = [halves(1.5 * identity - 0.5 * product) for product in products]
    terms = [split_dot(middles[b], get(inverse, b)) for b in tiles]
    scale = scales[...]
    root_scale = jnp.sqrt(jnp.float32(members - 1)) / jnp.sqrt(scale)
    inverse_scale = 1.0 / scale
    for b in tiles:
        half_step = jnp.sum(terms[b] * target[b][:1], axis=1, keepdims=True)
        shift = jnp.sum(terms[b] * half_step, axis=0, keepdims=True) * inverse_scale[b : b + 1]
        stack[pl.ds(b, members, stride=tile_rows), :] = terms[b] * root_scale[b : b + 1] + shift

    lane = lax.broadcasted_iota(jnp.int32, (tile_rows, tile_cols), 1)
    same = lax.rem(lane, tile_rows) == lax.broadcasted_iota(jnp.int32, lane.shape, 0)
    step = 128
    for first in range(0, deep, step):
        wide = jnp.dot(
            stack[first : first + step].astype(jnp.bfloat16),
            spots[...],
            preferred_element_type=jnp.float32,
        )
        for left in range(0, deep, tile_cols):
            block = wide[:, left : left + tile_cols].reshape(-1, tile_rows, tile_cols)
            big[first : first + step, left : left + tile_cols] = (
                jnp.where(same[None], block, 0.0).reshape(step, tile_cols).astype(jnp.bfloat16)
            )

    def send(pair):
        return pltpu.make_async_copy(
            result.at[:, pl.ds(pair * 2, 2)], out_ref.at[:, pl.ds(pair * 2, 2)], out_sem.at[pair]
        )

    @pl.loop(0, levels_n // 2, unroll=4)
    def _(pair):
        f = pair * 2
        right = jnp.concatenate([dev[f], dev[f + 1]], axis=1)
        update = jnp.dot(big[...], right, preferred_element_type=jnp.float32)
        for half in range(2):
            block = update[:, half * tile_cols : (half + 1) * tile_cols].reshape(
                members, tile_rows, tile_cols
            )
            result[:, f + half] = (block + mean[f + half][None]).astype(jnp.bfloat16)
        send(pair).start()

    @pl.loop(0, levels_n // 2)
    def _(pair):
        send(pair).wait()


def per_device(
    ensemble,
    obs_interp,
    obs_start,
    obs_levels,
    obs_values,
    obs_weight,
    obs_rows,
    obs_count,
    local_mask,
):
    lat_n = lax.axis_size("lat")
    lon_n = lax.axis_size("lon")
    total = lat_n * lon_n
    share, grid_rows, grid_cols = ensemble.shape
    tile_rows = grid_rows // lat_n
    tile_cols = grid_cols // lon_n
    slots_n, levels_n, obs_n = obs_levels.shape[2:]
    members = share * total // levels_n
    group = math.lcm(share, levels_n) // share
    groups = total // group
    span, width = members // 2 + 8, -(-members // 128) * 128
    plan = (lat_n, lon_n, share, tile_rows, tile_cols, levels_n, members, group)
    hbm = pl.BlockSpec(memory_space=pltpu.HBM)
    smem = pl.BlockSpec(memory_space=pltpu.SMEM)
    state, slots = pl.pallas_call(
        functools.partial(gather_kernel, plan),
        out_shape=(
            jax.ShapeDtypeStruct((share * total, tile_rows, tile_cols), jnp.bfloat16),
            jax.ShapeDtypeStruct((9, span, width), jnp.float32),
        ),
        in_specs=[hbm] * 6 + [smem] * 2,
        out_specs=(hbm, hbm),
        scratch_shapes=[pltpu.VMEM((share * total, tile_rows, tile_cols), jnp.bfloat16)]
        + [
            pltpu.VMEM(array.shape, array.dtype)
            for array in (obs_interp, obs_start, obs_levels, obs_values, obs_weight)
        ]
        + [
            pltpu.VMEM((slots_n, tile_cols, obs_n), jnp.bfloat16),
            pltpu.VMEM((tile_rows, group * share, tile_cols), jnp.bfloat16),
            pltpu.VMEM((group * share * tile_rows, tile_cols), jnp.float32),
            pltpu.VMEM((members * slots_n, obs_n), jnp.float32),
            pltpu.VMEM((3, span, width), jnp.float32),
            pltpu.VMEM((3, span, width), jnp.float32),
            pltpu.SemaphoreType.DMA((total,)),
            pltpu.SemaphoreType.DMA((total,)),
            pltpu.SemaphoreType.DMA((3,)),
            pltpu.SemaphoreType.DMA((3,)),
            pltpu.SemaphoreType.DMA((2,)),
            pltpu.SemaphoreType.DMA((2,)),
            pltpu.SemaphoreType.DMA((3,)),
            pltpu.SemaphoreType.DMA((3,)),
            pltpu.SemaphoreType.DMA((5,)),
            pltpu.SemaphoreType.DMA((groups,)),
        ],
        compiler_params=pltpu.CompilerParams(
            collective_id=0, has_side_effects=True, vmem_limit_bytes=60 * 1024 * 1024
        ),
    )(
        ensemble,
        obs_interp,
        obs_start,
        obs_levels,
        obs_values,
        obs_weight,
        obs_rows.reshape(-1),
        obs_count.reshape(-1),
    )
    tile_state = state.reshape(members, levels_n, tile_rows, tile_cols)
    deep = members * tile_rows
    pairs = (tile_rows, 2, members, width)
    return pl.pallas_call(
        functools.partial(
            analysis_kernel, (members, levels_n, tile_rows, tile_cols, NS_ITERS)
        ),
        out_shape=jax.ShapeDtypeStruct(tile_state.shape, jnp.bfloat16),
        in_specs=[hbm, hbm, hbm],
        out_specs=hbm,
        scratch_shapes=[
            pltpu.VMEM(tile_state.shape, jnp.bfloat16),
            pltpu.VMEM(slots.shape, jnp.float32),
            pltpu.VMEM(local_mask.shape, jnp.int32),
            pltpu.VMEM((9, tile_rows, width), jnp.float32),
            pltpu.VMEM(pairs, jnp.bfloat16),
            pltpu.VMEM(pairs, jnp.bfloat16),
            pltpu.VMEM((tile_rows, width), jnp.float32),
            pltpu.VMEM((tile_rows, 8, width), jnp.float32),
            pltpu.VMEM((deep, width), jnp.float32),
            pltpu.VMEM((width, deep), jnp.bfloat16),
            pltpu.VMEM((deep, deep), jnp.bfloat16),
            pltpu.VMEM((levels_n, deep, tile_cols), jnp.bfloat16),
            pltpu.VMEM((levels_n, tile_rows, tile_cols), jnp.float32),
            pltpu.VMEM(tile_state.shape, jnp.bfloat16),
            pltpu.SemaphoreType.DMA((NS_ITERS - 2,)),
            pltpu.SemaphoreType.DMA,
            pltpu.SemaphoreType.DMA,
            pltpu.SemaphoreType.DMA((levels_n // 2,)),
        ],
        compiler_params=pltpu.CompilerParams(vmem_limit_bytes=60 * 1024 * 1024),
    )(tile_state, slots, local_mask)


def solution(mesh):
    placed = (
        P(("lat", "lon"), None, None),
        P("lat", "lon", None, None, None),
        P("lat", "lon", None, None),
        P("lat", "lon", None, None, None),
        P("lat", "lon", None, None),
        P("lat", "lon", None, None),
        P("lat", "lon", None),
        P("lat", "lon"),
        P("lat", "lon", None, None),
    )
    return jax.shard_map(
        per_device,
        mesh=mesh,
        in_specs=placed,
        out_specs=P(None, None, "lat", "lon"),
        check_vma=False,
    )
```

```python
import functools
import math

import jax
import jax.numpy as jnp
from jax import lax
from jax.experimental import pallas as pl
from jax.experimental.pallas import tpu as pltpu
from jax.sharding import PartitionSpec as P

NS_ITERS = 6
MESH = pl.DeviceIdType.MESH


def flip(index, by, size):
    total, bit = 0, 1
    while bit < size:
        total += lax.rem(lax.div(index, bit) + lax.div(by, bit), 2) * bit
        bit *= 2
    return total


def gather_kernel(
    plan,
    ens_ref,
    interp_in,
    starts_in,
    levels_in,
    values_in,
    weights_in,
    rows_ref,
    count_ref,
    state_out,
    slots_out,
    state_ref,
    interp_ref,
    starts_ref,
    levels_ref,
    values_ref,
    weights_ref,
    dense,
    by_row,
    wide,
    obs,
    near,
    nothing,
    send_sem,
    recv_sem,
    near_send,
    near_recv,
    slot_send,
    slot_recv,
    polar_send,
    polar_recv,
    load_sem,
    hand_sem,
):
    lat_n, lon_n, share, tile_rows, tile_cols, levels_n, members, group = plan
    total = lat_n * lon_n
    packs = lon_n // group
    group_rows = group * share
    group_members = group_rows // levels_n
    slots_n, stencil = interp_ref.shape[2:4]
    lat, lon = lax.axis_index("lat"), lax.axis_index("lon")
    me = lat * lon_n + lon
    pack, place = lax.div(lon, group), lax.rem(lon, group)

    barrier = pltpu.get_barrier_semaphore()

    @pl.loop(1, total)
    def _(step):
        peer = lax.rem(me + step, total)
        pl.semaphore_signal(
            barrier,
            inc=1,
            device_id={"lat": peer // lon_n, "lon": lax.rem(peer, lon_n)},
            device_id_type=MESH,
        )

    pl.semaphore_wait(barrier, total - 1)

    def tile_copy(to_lat, to_lon, source):
        return pltpu.make_async_remote_copy(
            src_ref=ens_ref.at[
                :,
                pl.ds(pl.multiple_of(to_lat * tile_rows, tile_rows), tile_rows),
                pl.ds(pl.multiple_of(to_lon * tile_cols, tile_cols), tile_cols),
            ],
            dst_ref=state_ref.at[pl.ds(source * share, share)],
            send_sem=send_sem.at[to_lat * lon_n + to_lon],
            recv_sem=recv_sem.at[source],
            device_id={"lat": to_lat, "lon": to_lon},
            device_id_type=MESH,
        )

    def turn(t):
        far, step, g = lax.rem(t, 2), lax.rem(lax.div(t, 2), lat_n), lax.div(t, 2 * lat_n)
        back = lat_n - 1 - step
        turned = lax.div(g + packs - 1, packs) * (1 - far) + far
        by_lat = turned * back + (1 - turned) * step
        by_pack = far * (packs // 2) + g
        return flip(lat, by_lat, lat_n), flip(pack, by_pack, packs)

    own = pltpu.make_async_copy(
        ens_ref.at[
            :,
            pl.ds(pl.multiple_of(lat * tile_rows, tile_rows), tile_rows),
            pl.ds(pl.multiple_of(lon * tile_cols, tile_cols), tile_cols),
        ],
        state_ref.at[pl.ds(me * share, share)],
        recv_sem.at[me],
    )
    own.start()

    @pl.loop(0, lat_n * packs // 2)
    def _(step):
        @pl.loop(0, group)
        def _(i):
            for t in (step * 2 + 1, step * 2):
                to_lat, to_pack = turn(t)
                to_lon = to_pack * group + lax.rem(place + i, group)

                @pl.when(to_lat * lon_n + to_lon != me)
                def _():
                    tile_copy(to_lat, to_lon, me).start()

    loads = [
        pltpu.make_async_copy(source, target, load_sem.at[i])
        for i, (source, target) in enumerate(
            [
                (interp_in, interp_ref),
                (starts_in, starts_ref),
                (levels_in, levels_ref),
                (values_in, values_ref),
                (weights_in, weights_ref),
            ]
        )
    ]
    for copy in loads:
        copy.start()
    for copy in loads:
        copy.wait()

    last = lat_n - 1
    outside = pltpu.make_async_copy(nothing, slots_out.at[pl.ds(6, 3)], load_sem.at[2])

    @pl.when(lat == last)
    def _():
        nothing[...] = jnp.zeros_like(nothing)
        outside.start()

    cells = lax.broadcasted_iota(jnp.int32, (tile_cols, starts_ref.shape[-1]), 0)

    @pl.loop(0, slots_n, unroll=4)
    def _(j):
        first = starts_ref[0, 0, pl.ds(j, 1), :]
        taps = interp_ref[0, 0, j].astype(jnp.float32)
        offset = cells - first
        grid = jnp.zeros(cells.shape, jnp.float32)
        for p in range(stencil):
            grid = jnp.where(offset == p, taps[p : p + 1, :], grid)
        dense[j] = grid.astype(jnp.bfloat16)

    def hand_on(which):
        piece = pl.ds(which * group_rows, group_rows)
        return pltpu.make_async_copy(state_ref.at[piece], state_out.at[piece], hand_sem.at[which])

    def take_group(which):
        base = which * group_rows

        @pl.loop(0, group)
        def _(i):
            source = which * group + i
            tile_copy(source // lon_n, lax.rem(source, lon_n), source).wait_recv()

        hand_on(which).start()

        @pl.loop(0, group_members)
        def _(i):
            piece = state_ref[pl.ds(base + i * levels_n, levels_n)].astype(jnp.float32)
            span = levels_n * tile_rows
            wide[pl.ds(pl.multiple_of(i * span, span), span), :] = piece.reshape(span, tile_cols)

        for r in range(tile_rows):
            by_row[r] = wide[pl.ds(r, group_rows, stride=tile_rows), :].astype(jnp.bfloat16)

        first = which * group_members * (slots_n + 1)

        @pl.loop(0, slots_n, unroll=slots_n)
        def _(j):
            product = jnp.dot(by_row[rows_ref[j]], dense[j], preferred_element_type=jnp.float32)
            level = levels_ref[0, 0, j].astype(jnp.float32)
            obs[pl.ds(first + j, group_members, stride=slots_n + 1), :] = jnp.sum(
                product.reshape(group_members, levels_n, product.shape[1]) * level[None], axis=1
            )

    @pl.loop(0, lat_n * packs)
    def _(t):
        from_lat, from_pack = turn(t)
        take_group(from_lat * packs + from_pack)

    span, width = near.shape[1:]
    half = members // 2
    blank = jnp.zeros((width - members - half, tile_cols), jnp.float32)

    def add_blocks(pair, carry):
        lefts, rights = [], []
        for i in range(2):
            j = pair * 2 + i
            block = obs[pl.ds(j, members, stride=slots_n + 1), :]
            mean = jnp.sum(block, axis=0, keepdims=True) / members
            dev = block - mean
            innov = values_ref[0, 0, pl.ds(j, 1), :] - mean
            weight = weights_ref[0, 0, pl.ds(j, 1), :]
            live = jnp.where(jnp.full(weight.shape, j, jnp.int32) < count_ref[0], weight, 0.0)
            tail = jnp.broadcast_to(innov, (8, tile_cols))
            lefts.append(jnp.concatenate([dev, tail], axis=0).astype(jnp.bfloat16))
            heavy = dev * live
            rights.append(
                jnp.concatenate([heavy, heavy[half:], blank], axis=0).astype(jnp.bfloat16)
            )
        return carry + lax.dot_general(
            jnp.concatenate(lefts, axis=1),
            jnp.concatenate(rights, axis=1),
            (((1,), (1,)), ((), ())),
            preferred_element_type=jnp.float32,
        )

    summed = lax.fori_loop(
        0, slots_n // 2, add_blocks, jnp.zeros((members + 8, width), jnp.float32), unroll=slots_n // 2
    )
    lane = lax.broadcasted_iota(jnp.int32, (half, width), 1)
    near[1, :half] = jnp.where(lane < members, summed[:half], summed[half:members])
    near[1, half:] = summed[members:]

    def pass_on(source, target, sems, i, to_lat, to_lon):
        send, recv = sems
        return pltpu.make_async_remote_copy(
            src_ref=source,
            dst_ref=target,
            send_sem=send.at[i],
            recv_sem=recv.at[i],
            device_id={"lat": to_lat, "lon": to_lon},
            device_id_type=MESH,
        )

    east, west = lax.rem(lon + 1, lon_n), lax.rem(lon + lon_n - 1, lon_n)
    across = lax.rem(lon + lon_n // 2, lon_n)
    first, second = (near_send, near_recv), (slot_send, slot_recv)
    polar = (polar_send, polar_recv)
    row_mates = [
        pass_on(near.at[1], near.at[0], first, 0, lat, east),
        pass_on(near.at[1], near.at[2], first, 2, lat, west),
    ]
    over_pole = [
        pass_on(near.at[1], slots_out.at[s], polar, s, lat, lax.rem(across + lon_n + s - 1, lon_n))
        for s in range(3)
    ]
    south = pass_on(near, slots_out.at[pl.ds(0, 3)], second, 0, lat + 1, lon)
    north = pass_on(near, slots_out.at[pl.ds(6, 3)], second, 1, lat - 1, lon)
    keep_near = pltpu.make_async_copy(near, slots_out.at[pl.ds(3, 3)], load_sem.at[0])

    @pl.when(lat == 0)
    def _():
        for copy in over_pole:
            copy.start()

    for copy in row_mates:
        copy.start()

    for copy in row_mates:
        copy.wait_recv()

    @pl.when(lat < last)
    def _():
        south.start()

    @pl.when(lat > 0)
    def _():
        north.start()

    keep_near.start()

    @pl.loop(0, total)
    def _(peer):
        @pl.when(peer != me)
        def _():
            tile_copy(peer // lon_n, lax.rem(peer, lon_n), me).wait_send()

    @pl.loop(0, total // group)
    def _(which):
        hand_on(which).wait()

    for copy in row_mates:
        copy.wait_send()
    keep_near.wait()

    @pl.when(lat == 0)
    def _():
        for copy in over_pole:
            copy.wait()

    @pl.when(lat > 0)
    def _():
        south.wait_recv()
        north.wait_send()

    @pl.when(lat < last)
    def _():
        south.wait_send()
        north.wait_recv()

    @pl.when(lat == last)
    def _():
        outside.wait()


def halves(x):
    high = x.astype(jnp.bfloat16)
    return high, (x - high.astype(jnp.float32)).astype(jnp.bfloat16)


def split_dot(left, right):
    left_high, left_low = left
    right_high, right_low = right
    members, width = right_high.shape
    blank = jnp.zeros((width - members, 2 * width), jnp.bfloat16)
    top = jnp.concatenate([right_high, right_low], axis=1)
    low = jnp.concatenate([right_high, jnp.zeros_like(right_low)], axis=1)
    out = jnp.dot(
        jnp.concatenate([left_high, left_low], axis=1),
        jnp.concatenate([top, blank, low, blank], axis=0),
        preferred_element_type=jnp.float32,
    )
    return out[:, :width] + out[:, width:]


def analysis_kernel(
    plan,
    state_in,
    slots_in,
    mask_in,
    out_ref,
    state,
    slots,
    mask,
    chosen,
    root,
    inverse,
    scales,
    target,
    stack,
    spots,
    big,
    dev,
    mean,
    result,
    state_sem,
    slot_sem,
    mask_sem,
    out_sem,
):
    members, levels_n, tile_rows, tile_cols, ns_iters = plan
    width = slots.shape[2]
    deep = members * tile_rows
    parts = ns_iters - 2
    per = levels_n // parts
    tiles = range(tile_rows)

    load_mask = pltpu.make_async_copy(mask_in, mask, mask_sem)
    load_mask.start()
    load_slots = pltpu.make_async_copy(slots_in, slots, slot_sem)
    load_slots.start()

    def load_state(i):
        piece = pl.ds(i * per, per)
        return pltpu.make_async_copy(state_in.at[:, piece], state.at[:, piece], state_sem.at[i])

    for i in range(parts):
        load_state(i).start()

    rows = lax.broadcasted_iota(jnp.int32, (members, width), 0)
    cols = lax.broadcasted_iota(jnp.int32, (members, width), 1)
    identity = jnp.where(rows == cols, 1.0, 0.0)
    source = lax.broadcasted_iota(jnp.int32, (width, deep), 0)
    spot = lax.broadcasted_iota(jnp.int32, (width, deep), 1) - source * tile_rows
    spots[...] = jnp.where((spot >= 0) & (spot < tile_rows), 1.0, 0.0).astype(jnp.bfloat16)

    load_mask.wait()
    use = mask[0, 0].astype(jnp.float32)
    for slot in range(9):
        chosen[slot] = jnp.broadcast_to(use[:, slot : slot + 1], chosen.shape[1:])

    load_slots.wait()

    half = members // 2
    lane = cols[:half]
    real = cols < members
    empty = jnp.zeros((width - half, width), jnp.float32)
    systems, totals = [], []
    for b in tiles:
        summed = chosen[0, b : b + 1] * slots[0]
        for slot in range(1, 9):
            summed += chosen[slot, b : b + 1] * slots[slot]
        target[b] = summed[half:]
        top = summed[:half]
        turned = pltpu.roll(top, width - half, 1)
        across = jnp.concatenate([turned, empty], axis=0).T[:half]
        bottom = jnp.where(lane < half, across, turned)
        whole = jnp.where(real, jnp.concatenate([top, bottom], axis=0), 0.0)
        system = (members - 1) * identity + whole
        totals.append(jnp.sum(system * system, axis=0, keepdims=True))
        systems.append(system)
    scale = jnp.sqrt(jnp.sum(jnp.concatenate(totals, axis=0), axis=1, keepdims=True))
    scales[...] = jnp.broadcast_to(scale, scales.shape)
    inverse_scale = 1.0 / scale
    roots = [systems[b] * inverse_scale[b : b + 1] for b in tiles]
    middles = [halves(1.5 * identity - 0.5 * roots[b]) for b in tiles]

    def put(ref, b, pair):
        ref[b, 0], ref[b, 1] = pair

    def get(ref, b):
        return ref[b, 0], ref[b, 1]

    for b in tiles:
        put(inverse, b, middles[b])
        put(root, b, halves(split_dot(halves(roots[b]), middles[b])))

    @pl.loop(0, parts)
    def _(repeat):
        products = [split_dot(get(inverse, b), get(root, b)) for b in tiles]
        load_state(repeat).wait()
        for i in range(per):
            f = repeat * per + i
            cell = state[:, f].astype(jnp.float32)
            average = jnp.sum(cell, axis=0) / members
            mean[f] = average
            dev[f] = (cell - average[None]).reshape(deep, tile_cols).astype(jnp.bfloat16)
        middles = [halves(1.5 * identity - 0.5 * product) for product in products]
        new_root = [split_dot(get(root, b), middles[b]) for b in tiles]
        new_inverse = [split_dot(middles[b], get(inverse, b)) for b in tiles]
        for b in tiles:
            put(root, b, halves(new_root[b]))
            put(inverse, b, halves(new_inverse[b]))

    products = [split_dot(get(inverse, b), get(root, b)) for b in tiles]
    middles = [halves(1.5 * identity - 0.5 * product) for product in products]
    terms = [split_dot(middles[b], get(inverse, b)) for b in tiles]
    scale = scales[...]
    root_scale = jnp.sqrt(jnp.float32(members - 1)) / jnp.sqrt(scale)
    inverse_scale = 1.0 / scale
    for b in tiles:
        half_step = jnp.sum(terms[b] * target[b][:1], axis=1, keepdims=True)
        shift = jnp.sum(terms[b] * half_step, axis=0, keepdims=True) * inverse_scale[b : b + 1]
        stack[pl.ds(b, members, stride=tile_rows), :] = terms[b] * root_scale[b : b + 1] + shift

    lane = lax.broadcasted_iota(jnp.int32, (tile_rows, tile_cols), 1)
    same = lax.rem(lane, tile_rows) == lax.broadcasted_iota(jnp.int32, lane.shape, 0)
    step = 128
    for first in range(0, deep, step):
        wide = jnp.dot(
            stack[first : first + step].astype(jnp.bfloat16),
            spots[...],
            preferred_element_type=jnp.float32,
        )
        for left in range(0, deep, tile_cols):
            block = wide[:, left : left + tile_cols].reshape(-1, tile_rows, tile_cols)
            big[first : first + step, left : left + tile_cols] = (
                jnp.where(same[None], block, 0.0).reshape(step, tile_cols).astype(jnp.bfloat16)
            )

    def send(pair):
        return pltpu.make_async_copy(
            result.at[:, pl.ds(pair * 2, 2)], out_ref.at[:, pl.ds(pair * 2, 2)], out_sem.at[pair]
        )

    @pl.loop(0, levels_n // 2, unroll=4)
    def _(pair):
        f = pair * 2
        right = jnp.concatenate([dev[f], dev[f + 1]], axis=1)
        update = jnp.dot(big[...], right, preferred_element_type=jnp.float32)
        for half in range(2):
            block = update[:, half * tile_cols : (half + 1) * tile_cols].reshape(
                members, tile_rows, tile_cols
            )
            result[:, f + half] = (block + mean[f + half][None]).astype(jnp.bfloat16)
        send(pair).start()

    @pl.loop(0, levels_n // 2)
    def _(pair):
        send(pair).wait()


def per_device(
    ensemble,
    obs_interp,
    obs_start,
    obs_levels,
    obs_values,
    obs_weight,
    obs_rows,
    obs_count,
    local_mask,
):
    lat_n = lax.axis_size("lat")
    lon_n = lax.axis_size("lon")
    total = lat_n * lon_n
    share, grid_rows, grid_cols = ensemble.shape
    tile_rows = grid_rows // lat_n
    tile_cols = grid_cols // lon_n
    slots_n, levels_n, obs_n = obs_levels.shape[2:]
    members = share * total // levels_n
    group = math.lcm(share, levels_n) // share
    groups = total // group
    span, width = members // 2 + 8, -(-members // 128) * 128
    plan = (lat_n, lon_n, share, tile_rows, tile_cols, levels_n, members, group)
    hbm = pl.BlockSpec(memory_space=pltpu.HBM)
    smem = pl.BlockSpec(memory_space=pltpu.SMEM)
    state, slots = pl.pallas_call(
        functools.partial(gather_kernel, plan),
        out_shape=(
            jax.ShapeDtypeStruct((share * total, tile_rows, tile_cols), jnp.bfloat16),
            jax.ShapeDtypeStruct((9, span, width), jnp.float32),
        ),
        in_specs=[hbm] * 6 + [smem] * 2,
        out_specs=(hbm, hbm),
        scratch_shapes=[pltpu.VMEM((share * total, tile_rows, tile_cols), jnp.bfloat16)]
        + [
            pltpu.VMEM(array.shape, array.dtype)
            for array in (obs_interp, obs_start, obs_levels, obs_values, obs_weight)
        ]
        + [
            pltpu.VMEM((slots_n, tile_cols, obs_n), jnp.bfloat16),
            pltpu.VMEM((tile_rows, group * share, tile_cols), jnp.bfloat16),
            pltpu.VMEM((group * share * tile_rows, tile_cols), jnp.float32),
            pltpu.VMEM((members * (slots_n + 1), obs_n), jnp.float32),
            pltpu.VMEM((3, span, width), jnp.float32),
            pltpu.VMEM((3, span, width), jnp.float32),
            pltpu.SemaphoreType.DMA((total,)),
            pltpu.SemaphoreType.DMA((total,)),
            pltpu.SemaphoreType.DMA((3,)),
            pltpu.SemaphoreType.DMA((3,)),
            pltpu.SemaphoreType.DMA((2,)),
            pltpu.SemaphoreType.DMA((2,)),
            pltpu.SemaphoreType.DMA((3,)),
            pltpu.SemaphoreType.DMA((3,)),
            pltpu.SemaphoreType.DMA((5,)),
            pltpu.SemaphoreType.DMA((groups,)),
        ],
        compiler_params=pltpu.CompilerParams(
            collective_id=0, has_side_effects=True, vmem_limit_bytes=60 * 1024 * 1024
        ),
    )(
        ensemble,
        obs_interp,
        obs_start,
        obs_levels,
        obs_values,
        obs_weight,
        obs_rows.reshape(-1),
        obs_count.reshape(-1),
    )
    tile_state = state.reshape(members, levels_n, tile_rows, tile_cols)
    deep = members * tile_rows
    pairs = (tile_rows, 2, members, width)
    return pl.pallas_call(
        functools.partial(
            analysis_kernel, (members, levels_n, tile_rows, tile_cols, NS_ITERS)
        ),
        out_shape=jax.ShapeDtypeStruct(tile_state.shape, jnp.bfloat16),
        in_specs=[hbm, hbm, hbm],
        out_specs=hbm,
        scratch_shapes=[
            pltpu.VMEM(tile_state.shape, jnp.bfloat16),
            pltpu.VMEM(slots.shape, jnp.float32),
            pltpu.VMEM(local_mask.shape, jnp.int32),
            pltpu.VMEM((9, tile_rows, width), jnp.float32),
            pltpu.VMEM(pairs, jnp.bfloat16),
            pltpu.VMEM(pairs, jnp.bfloat16),
            pltpu.VMEM((tile_rows, width), jnp.float32),
            pltpu.VMEM((tile_rows, 8, width), jnp.float32),
            pltpu.VMEM((deep, width), jnp.float32),
            pltpu.VMEM((width, deep), jnp.bfloat16),
            pltpu.VMEM((deep, deep), jnp.bfloat16),
            pltpu.VMEM((levels_n, deep, tile_cols), jnp.bfloat16),
            pltpu.VMEM((levels_n, tile_rows, tile_cols), jnp.float32),
            pltpu.VMEM(tile_state.shape, jnp.bfloat16),
            pltpu.SemaphoreType.DMA((NS_ITERS - 2,)),
            pltpu.SemaphoreType.DMA,
            pltpu.SemaphoreType.DMA,
            pltpu.SemaphoreType.DMA((levels_n // 2,)),
        ],
        compiler_params=pltpu.CompilerParams(vmem_limit_bytes=60 * 1024 * 1024),
    )(tile_state, slots, local_mask)


def solution(mesh):
    placed = (
        P(("lat", "lon"), None, None),
        P("lat", "lon", None, None, None),
        P("lat", "lon", None, None),
        P("lat", "lon", None, None, None),
        P("lat", "lon", None, None),
        P("lat", "lon", None, None),
        P("lat", "lon", None),
        P("lat", "lon"),
        P("lat", "lon", None, None),
    )
    return jax.shard_map(
        per_device,
        mesh=mesh,
        in_specs=placed,
        out_specs=P(None, None, "lat", "lon"),
        check_vma=False,
    )
```

```python
import functools
import math

import jax
import jax.numpy as jnp
from jax import lax
from jax.experimental import pallas as pl
from jax.experimental.pallas import tpu as pltpu
from jax.sharding import PartitionSpec as P

NS_ITERS = 6
MESH = pl.DeviceIdType.MESH


def flip(index, by, size):
    total, bit = 0, 1
    while bit < size:
        total += lax.rem(lax.div(index, bit) + lax.div(by, bit), 2) * bit
        bit *= 2
    return total


def gather_kernel(
    plan,
    ens_ref,
    interp_in,
    starts_in,
    levels_in,
    values_in,
    weights_in,
    rows_ref,
    count_ref,
    state_out,
    slots_out,
    state_ref,
    interp_ref,
    starts_ref,
    levels_ref,
    values_ref,
    weights_ref,
    dense,
    by_row,
    wide,
    obs,
    near,
    nothing,
    send_sem,
    recv_sem,
    near_send,
    near_recv,
    slot_send,
    slot_recv,
    polar_send,
    polar_recv,
    load_sem,
    hand_sem,
):
    lat_n, lon_n, share, tile_rows, tile_cols, levels_n, members, group = plan
    total = lat_n * lon_n
    packs = lon_n // group
    group_rows = group * share
    group_members = group_rows // levels_n
    slots_n, stencil = interp_ref.shape[2:4]
    lat, lon = lax.axis_index("lat"), lax.axis_index("lon")
    me = lat * lon_n + lon
    pack, place = lax.div(lon, group), lax.rem(lon, group)

    barrier = pltpu.get_barrier_semaphore()

    @pl.loop(1, total)
    def _(step):
        peer = lax.rem(me + step, total)
        pl.semaphore_signal(
            barrier,
            inc=1,
            device_id={"lat": peer // lon_n, "lon": lax.rem(peer, lon_n)},
            device_id_type=MESH,
        )

    pl.semaphore_wait(barrier, total - 1)

    def tile_copy(to_lat, to_lon, source):
        return pltpu.make_async_remote_copy(
            src_ref=ens_ref.at[
                :,
                pl.ds(pl.multiple_of(to_lat * tile_rows, tile_rows), tile_rows),
                pl.ds(pl.multiple_of(to_lon * tile_cols, tile_cols), tile_cols),
            ],
            dst_ref=state_ref.at[pl.ds(source * share, share)],
            send_sem=send_sem.at[to_lat * lon_n + to_lon],
            recv_sem=recv_sem.at[source],
            device_id={"lat": to_lat, "lon": to_lon},
            device_id_type=MESH,
        )

    def turn(t):
        far, step, g = lax.rem(t, 2), lax.rem(lax.div(t, 2), lat_n), lax.div(t, 2 * lat_n)
        back = lat_n - 1 - step
        turned = lax.div(g + packs - 1, packs) * (1 - far) + far
        by_lat = turned * back + (1 - turned) * step
        by_pack = far * (packs // 2) + g
        return flip(lat, by_lat, lat_n), flip(pack, by_pack, packs)

    own = pltpu.make_async_copy(
        ens_ref.at[
            :,
            pl.ds(pl.multiple_of(lat * tile_rows, tile_rows), tile_rows),
            pl.ds(pl.multiple_of(lon * tile_cols, tile_cols), tile_cols),
        ],
        state_ref.at[pl.ds(me * share, share)],
        recv_sem.at[me],
    )
    own.start()

    @pl.loop(0, lat_n * packs // 2)
    def _(step):
        @pl.loop(0, group)
        def _(i):
            for t in (step * 2 + 1, step * 2):
                to_lat, to_pack = turn(t)
                to_lon = to_pack * group + lax.rem(place + i, group)

                @pl.when(to_lat * lon_n + to_lon != me)
                def _():
                    tile_copy(to_lat, to_lon, me).start()

    loads = [
        pltpu.make_async_copy(source, target, load_sem.at[i])
        for i, (source, target) in enumerate(
            [
                (interp_in, interp_ref),
                (starts_in, starts_ref),
                (levels_in, levels_ref),
                (values_in, values_ref),
                (weights_in, weights_ref),
            ]
        )
    ]
    for copy in loads:
        copy.start()
    for copy in loads:
        copy.wait()

    last = lat_n - 1
    outside = pltpu.make_async_copy(nothing, slots_out.at[pl.ds(6, 3)], load_sem.at[2])

    @pl.when(lat == last)
    def _():
        nothing[...] = jnp.zeros_like(nothing)
        outside.start()

    cells = lax.broadcasted_iota(jnp.int32, (tile_cols, starts_ref.shape[-1]), 0)

    @pl.loop(0, slots_n, unroll=4)
    def _(j):
        first = starts_ref[0, 0, pl.ds(j, 1), :]
        taps = interp_ref[0, 0, j].astype(jnp.float32)
        offset = cells - first
        grid = jnp.zeros(cells.shape, jnp.float32)
        for p in range(stencil):
            grid = jnp.where(offset == p, taps[p : p + 1, :], grid)
        dense[j] = grid.astype(jnp.bfloat16)

    def hand_on(which):
        piece = pl.ds(which * group_rows, group_rows)
        return pltpu.make_async_copy(state_ref.at[piece], state_out.at[piece], hand_sem.at[which])

    def take_group(which):
        base = which * group_rows

        @pl.loop(0, group)
        def _(i):
            source = which * group + i
            tile_copy(source // lon_n, lax.rem(source, lon_n), source).wait_recv()

        hand_on(which).start()

        @pl.loop(0, group_members)
        def _(i):
            piece = state_ref[pl.ds(base + i * levels_n, levels_n)].astype(jnp.float32)
            span = levels_n * tile_rows
            wide[pl.ds(pl.multiple_of(i * span, span), span), :] = piece.reshape(span, tile_cols)

        for r in range(tile_rows):
            by_row[r] = wide[pl.ds(r, group_rows, stride=tile_rows), :].astype(jnp.bfloat16)

        first = which * group_members * (slots_n + 1)

        @pl.loop(0, slots_n, unroll=slots_n)
        def _(j):
            product = jnp.dot(by_row[rows_ref[j]], dense[j], preferred_element_type=jnp.float32)
            level = levels_ref[0, 0, j].astype(jnp.float32)
            obs[pl.ds(first + j, group_members, stride=slots_n + 1), :] = jnp.sum(
                product.reshape(group_members, levels_n, product.shape[1]) * level[None], axis=1
            )

    @pl.loop(0, lat_n * packs)
    def _(t):
        from_lat, from_pack = turn(t)
        take_group(from_lat * packs + from_pack)

    span, width = near.shape[1:]
    half = members // 2
    blank = jnp.zeros((width - members - half, tile_cols), jnp.float32)

    def add_blocks(pair, carry):
        lefts, rights = [], []
        for i in range(2):
            j = pair * 2 + i
            block = obs[pl.ds(j, members, stride=slots_n + 1), :]
            mean = jnp.sum(block, axis=0, keepdims=True) / members
            dev = block - mean
            innov = values_ref[0, 0, pl.ds(j, 1), :] - mean
            weight = weights_ref[0, 0, pl.ds(j, 1), :]
            live = jnp.where(jnp.full(weight.shape, j, jnp.int32) < count_ref[0], weight, 0.0)
            tail = jnp.broadcast_to(innov, (8, tile_cols))
            lefts.append(jnp.concatenate([dev, tail], axis=0).astype(jnp.bfloat16))
            heavy = dev * live
            rights.append(
                jnp.concatenate([heavy, heavy[half:], blank], axis=0).astype(jnp.bfloat16)
            )
        return carry + lax.dot_general(
            jnp.concatenate(lefts, axis=1),
            jnp.concatenate(rights, axis=1),
            (((1,), (1,)), ((), ())),
            preferred_element_type=jnp.float32,
        )

    summed = lax.fori_loop(
        0, slots_n // 2, add_blocks, jnp.zeros((members + 8, width), jnp.float32), unroll=slots_n // 2
    )
    lane = lax.broadcasted_iota(jnp.int32, (half, width), 1)
    near[1, :half] = jnp.where(lane < members, summed[:half], summed[half:members])
    near[1, half:] = summed[members:]

    def pass_on(source, target, sems, i, to_lat, to_lon):
        send, recv = sems
        return pltpu.make_async_remote_copy(
            src_ref=source,
            dst_ref=target,
            send_sem=send.at[i],
            recv_sem=recv.at[i],
            device_id={"lat": to_lat, "lon": to_lon},
            device_id_type=MESH,
        )

    east, west = lax.rem(lon + 1, lon_n), lax.rem(lon + lon_n - 1, lon_n)
    across = lax.rem(lon + lon_n // 2, lon_n)
    first, second = (near_send, near_recv), (slot_send, slot_recv)
    polar = (polar_send, polar_recv)
    row_mates = [
        pass_on(near.at[1], near.at[0], first, 0, lat, east),
        pass_on(near.at[1], near.at[2], first, 2, lat, west),
    ]
    over_pole = [
        pass_on(near.at[1], slots_out.at[s], polar, s, lat, lax.rem(across + lon_n + s - 1, lon_n))
        for s in range(3)
    ]
    south = pass_on(near, slots_out.at[pl.ds(0, 3)], second, 0, lat + 1, lon)
    north = pass_on(near, slots_out.at[pl.ds(6, 3)], second, 1, lat - 1, lon)
    keep_near = pltpu.make_async_copy(near, slots_out.at[pl.ds(3, 3)], load_sem.at[0])

    @pl.when(lat == 0)
    def _():
        for copy in over_pole:
            copy.start()

    for copy in row_mates:
        copy.start()

    for copy in row_mates:
        copy.wait_recv()

    @pl.when(lat < last)
    def _():
        south.start()

    @pl.when(lat > 0)
    def _():
        north.start()

    keep_near.start()

    @pl.loop(0, total)
    def _(peer):
        @pl.when(peer != me)
        def _():
            tile_copy(peer // lon_n, lax.rem(peer, lon_n), me).wait_send()

    @pl.loop(0, total // group)
    def _(which):
        hand_on(which).wait()

    for copy in row_mates:
        copy.wait_send()
    keep_near.wait()

    @pl.when(lat == 0)
    def _():
        for copy in over_pole:
            copy.wait()

    @pl.when(lat > 0)
    def _():
        south.wait_recv()
        north.wait_send()

    @pl.when(lat < last)
    def _():
        south.wait_send()
        north.wait_recv()

    @pl.when(lat == last)
    def _():
        outside.wait()


def halves(x):
    high = x.astype(jnp.bfloat16)
    return high, (x - high.astype(jnp.float32)).astype(jnp.bfloat16)


def split_dot(left, right):
    left_high, left_low = left
    right_high, right_low = right
    members, width = right_high.shape
    blank = jnp.zeros((width - members, 2 * width), jnp.bfloat16)
    top = jnp.concatenate([right_high, right_low], axis=1)
    low = jnp.concatenate([right_high, jnp.zeros_like(right_low)], axis=1)
    out = jnp.dot(
        jnp.concatenate([left_high, left_low], axis=1),
        jnp.concatenate([top, blank, low, blank], axis=0),
        preferred_element_type=jnp.float32,
    )
    return out[:, :width] + out[:, width:]


def analysis_kernel(
    plan,
    state_in,
    slots_in,
    mask_in,
    out_ref,
    state,
    slots,
    mask,
    chosen,
    root,
    inverse,
    scales,
    target,
    stack,
    spots,
    big,
    dev,
    mean,
    result,
    state_sem,
    slot_sem,
    mask_sem,
    out_sem,
):
    members, levels_n, tile_rows, tile_cols, ns_iters = plan
    width = slots.shape[2]
    deep = members * tile_rows
    parts = ns_iters - 2
    per = levels_n // parts
    tiles = range(tile_rows)

    load_mask = pltpu.make_async_copy(mask_in, mask, mask_sem)
    load_mask.start()
    load_slots = pltpu.make_async_copy(slots_in, slots, slot_sem)
    load_slots.start()

    def load_state(i):
        piece = pl.ds(i * per, per)
        return pltpu.make_async_copy(state_in.at[:, piece], state.at[:, piece], state_sem.at[i])


    rows = lax.broadcasted_iota(jnp.int32, (members, width), 0)
    cols = lax.broadcasted_iota(jnp.int32, (members, width), 1)
    identity = jnp.where(rows == cols, 1.0, 0.0)
    source = lax.broadcasted_iota(jnp.int32, (width, deep), 0)
    spot = lax.broadcasted_iota(jnp.int32, (width, deep), 1) - source * tile_rows
    spots[...] = jnp.where((spot >= 0) & (spot < tile_rows), 1.0, 0.0).astype(jnp.bfloat16)

    load_mask.wait()
    use = mask[0, 0].astype(jnp.float32)
    for slot in range(9):
        chosen[slot] = jnp.broadcast_to(use[:, slot : slot + 1], chosen.shape[1:])

    load_slots.wait()
    for i in range(parts):
        load_state(i).start()

    half = members // 2
    lane = cols[:half]
    real = cols < members
    empty = jnp.zeros((width - half, width), jnp.float32)
    systems, totals = [], []
    for b in tiles:
        summed = chosen[0, b : b + 1] * slots[0]
        for slot in range(1, 9):
            summed += chosen[slot, b : b + 1] * slots[slot]
        target[b] = summed[half:]
        top = summed[:half]
        turned = pltpu.roll(top, width - half, 1)
        across = jnp.concatenate([turned, empty], axis=0).T[:half]
        bottom = jnp.where(lane < half, across, turned)
        whole = jnp.where(real, jnp.concatenate([top, bottom], axis=0), 0.0)
        system = (members - 1) * identity + whole
        totals.append(jnp.sum(system * system, axis=0, keepdims=True))
        systems.append(system)
    scale = jnp.sqrt(jnp.sum(jnp.concatenate(totals, axis=0), axis=1, keepdims=True))
    scales[...] = jnp.broadcast_to(scale, scales.shape)
    inverse_scale = 1.0 / scale
    roots = [systems[b] * inverse_scale[b : b + 1] for b in tiles]
    middles = [halves(1.5 * identity - 0.5 * roots[b]) for b in tiles]

    def put(ref, b, pair):
        ref[b, 0], ref[b, 1] = pair

    def get(ref, b):
        return ref[b, 0], ref[b, 1]

    for b in tiles:
        put(inverse, b, middles[b])
        put(root, b, halves(split_dot(halves(roots[b]), middles[b])))

    @pl.loop(0, parts, unroll=parts)
    def _(repeat):
        products = [split_dot(get(inverse, b), get(root, b)) for b in tiles]
        load_state(repeat).wait()
        for i in range(per):
            f = repeat * per + i
            cell = state[:, f].astype(jnp.float32)
            average = jnp.sum(cell, axis=0) / members
            mean[f] = average
            dev[f] = (cell - average[None]).reshape(deep, tile_cols).astype(jnp.bfloat16)
        middles = [halves(1.5 * identity - 0.5 * product) for product in products]
        new_root = [split_dot(get(root, b), middles[b]) for b in tiles]
        new_inverse = [split_dot(middles[b], get(inverse, b)) for b in tiles]
        for b in tiles:
            put(root, b, halves(new_root[b]))
            put(inverse, b, halves(new_inverse[b]))

    products = [split_dot(get(inverse, b), get(root, b)) for b in tiles]
    middles = [halves(1.5 * identity - 0.5 * product) for product in products]
    terms = [split_dot(middles[b], get(inverse, b)) for b in tiles]
    scale = scales[...]
    root_scale = jnp.sqrt(jnp.float32(members - 1)) / jnp.sqrt(scale)
    inverse_scale = 1.0 / scale
    for b in tiles:
        half_step = jnp.sum(terms[b] * target[b][:1], axis=1, keepdims=True)
        shift = jnp.sum(terms[b] * half_step, axis=0, keepdims=True) * inverse_scale[b : b + 1]
        stack[pl.ds(b, members, stride=tile_rows), :] = terms[b] * root_scale[b : b + 1] + shift

    lane = lax.broadcasted_iota(jnp.int32, (tile_rows, tile_cols), 1)
    same = lax.rem(lane, tile_rows) == lax.broadcasted_iota(jnp.int32, lane.shape, 0)
    step = 128
    for first in range(0, deep, step):
        wide = jnp.dot(
            stack[first : first + step].astype(jnp.bfloat16),
            spots[...],
            preferred_element_type=jnp.float32,
        )
        for left in range(0, deep, tile_cols):
            block = wide[:, left : left + tile_cols].reshape(-1, tile_rows, tile_cols)
            big[first : first + step, left : left + tile_cols] = (
                jnp.where(same[None], block, 0.0).reshape(step, tile_cols).astype(jnp.bfloat16)
            )

    def send(pair):
        return pltpu.make_async_copy(
            result.at[:, pl.ds(pair * 2, 2)], out_ref.at[:, pl.ds(pair * 2, 2)], out_sem.at[pair]
        )

    @pl.loop(0, levels_n // 2, unroll=levels_n // 2)
    def _(pair):
        f = pair * 2
        right = jnp.concatenate([dev[f], dev[f + 1]], axis=1)
        update = jnp.dot(big[...], right, preferred_element_type=jnp.float32)
        for half in range(2):
            block = update[:, half * tile_cols : (half + 1) * tile_cols].reshape(
                members, tile_rows, tile_cols
            )
            result[:, f + half] = (block + mean[f + half][None]).astype(jnp.bfloat16)
        send(pair).start()

    @pl.loop(0, levels_n // 2)
    def _(pair):
        send(pair).wait()


def per_device(
    ensemble,
    obs_interp,
    obs_start,
    obs_levels,
    obs_values,
    obs_weight,
    obs_rows,
    obs_count,
    local_mask,
):
    lat_n = lax.axis_size("lat")
    lon_n = lax.axis_size("lon")
    total = lat_n * lon_n
    share, grid_rows, grid_cols = ensemble.shape
    tile_rows = grid_rows // lat_n
    tile_cols = grid_cols // lon_n
    slots_n, levels_n, obs_n = obs_levels.shape[2:]
    members = share * total // levels_n
    group = math.lcm(share, levels_n) // share
    groups = total // group
    span, width = members // 2 + 8, -(-members // 128) * 128
    plan = (lat_n, lon_n, share, tile_rows, tile_cols, levels_n, members, group)
    hbm = pl.BlockSpec(memory_space=pltpu.HBM)
    smem = pl.BlockSpec(memory_space=pltpu.SMEM)
    state, slots = pl.pallas_call(
        functools.partial(gather_kernel, plan),
        out_shape=(
            jax.ShapeDtypeStruct((share * total, tile_rows, tile_cols), jnp.bfloat16),
            jax.ShapeDtypeStruct((9, span, width), jnp.float32),
        ),
        in_specs=[hbm] * 6 + [smem] * 2,
        out_specs=(hbm, hbm),
        scratch_shapes=[pltpu.VMEM((share * total, tile_rows, tile_cols), jnp.bfloat16)]
        + [
            pltpu.VMEM(array.shape, array.dtype)
            for array in (obs_interp, obs_start, obs_levels, obs_values, obs_weight)
        ]
        + [
            pltpu.VMEM((slots_n, tile_cols, obs_n), jnp.bfloat16),
            pltpu.VMEM((tile_rows, group * share, tile_cols), jnp.bfloat16),
            pltpu.VMEM((group * share * tile_rows, tile_cols), jnp.float32),
            pltpu.VMEM((members * (slots_n + 1), obs_n), jnp.float32),
            pltpu.VMEM((3, span, width), jnp.float32),
            pltpu.VMEM((3, span, width), jnp.float32),
            pltpu.SemaphoreType.DMA((total,)),
            pltpu.SemaphoreType.DMA((total,)),
            pltpu.SemaphoreType.DMA((3,)),
            pltpu.SemaphoreType.DMA((3,)),
            pltpu.SemaphoreType.DMA((2,)),
            pltpu.SemaphoreType.DMA((2,)),
            pltpu.SemaphoreType.DMA((3,)),
            pltpu.SemaphoreType.DMA((3,)),
            pltpu.SemaphoreType.DMA((5,)),
            pltpu.SemaphoreType.DMA((groups,)),
        ],
        compiler_params=pltpu.CompilerParams(
            collective_id=0, has_side_effects=True, vmem_limit_bytes=60 * 1024 * 1024
        ),
    )(
        ensemble,
        obs_interp,
        obs_start,
        obs_levels,
        obs_values,
        obs_weight,
        obs_rows.reshape(-1),
        obs_count.reshape(-1),
    )
    tile_state = state.reshape(members, levels_n, tile_rows, tile_cols)
    deep = members * tile_rows
    pairs = (tile_rows, 2, members, width)
    return pl.pallas_call(
        functools.partial(
            analysis_kernel, (members, levels_n, tile_rows, tile_cols, NS_ITERS)
        ),
        out_shape=jax.ShapeDtypeStruct(tile_state.shape, jnp.bfloat16),
        in_specs=[hbm, hbm, hbm],
        out_specs=hbm,
        scratch_shapes=[
            pltpu.VMEM(tile_state.shape, jnp.bfloat16),
            pltpu.VMEM(slots.shape, jnp.float32),
            pltpu.VMEM(local_mask.shape, jnp.int32),
            pltpu.VMEM((9, tile_rows, width), jnp.float32),
            pltpu.VMEM(pairs, jnp.bfloat16),
            pltpu.VMEM(pairs, jnp.bfloat16),
            pltpu.VMEM((tile_rows, width), jnp.float32),
            pltpu.VMEM((tile_rows, 8, width), jnp.float32),
            pltpu.VMEM((deep, width), jnp.float32),
            pltpu.VMEM((width, deep), jnp.bfloat16),
            pltpu.VMEM((deep, deep), jnp.bfloat16),
            pltpu.VMEM((levels_n, deep, tile_cols), jnp.bfloat16),
            pltpu.VMEM((levels_n, tile_rows, tile_cols), jnp.float32),
            pltpu.VMEM(tile_state.shape, jnp.bfloat16),
            pltpu.SemaphoreType.DMA((NS_ITERS - 2,)),
            pltpu.SemaphoreType.DMA,
            pltpu.SemaphoreType.DMA,
            pltpu.SemaphoreType.DMA((levels_n // 2,)),
        ],
        compiler_params=pltpu.CompilerParams(vmem_limit_bytes=60 * 1024 * 1024),
    )(tile_state, slots, local_mask)


def solution(mesh):
    placed = (
        P(("lat", "lon"), None, None),
        P("lat", "lon", None, None, None),
        P("lat", "lon", None, None),
        P("lat", "lon", None, None, None),
        P("lat", "lon", None, None),
        P("lat", "lon", None, None),
        P("lat", "lon", None),
        P("lat", "lon"),
        P("lat", "lon", None, None),
    )
    return jax.shard_map(
        per_device,
        mesh=mesh,
        in_specs=placed,
        out_specs=P(None, None, "lat", "lon"),
        check_vma=False,
    )
```

```python
import functools
import math

import jax
import jax.numpy as jnp
from jax import lax
from jax.experimental import pallas as pl
from jax.experimental.pallas import tpu as pltpu
from jax.sharding import PartitionSpec as P

NS_ITERS = 6
MESH = pl.DeviceIdType.MESH


def flip(index, by, size):
    total, bit = 0, 1
    while bit < size:
        total += lax.rem(lax.div(index, bit) + lax.div(by, bit), 2) * bit
        bit *= 2
    return total


def gather_kernel(
    plan,
    ens_ref,
    interp_in,
    starts_in,
    levels_in,
    values_in,
    weights_in,
    rows_ref,
    count_ref,
    state_out,
    slots_out,
    state_ref,
    interp_ref,
    starts_ref,
    levels_ref,
    values_ref,
    weights_ref,
    dense,
    by_row,
    wide,
    obs,
    near,
    nothing,
    send_sem,
    recv_sem,
    near_send,
    near_recv,
    slot_send,
    slot_recv,
    polar_send,
    polar_recv,
    load_sem,
    hand_sem,
):
    lat_n, lon_n, share, tile_rows, tile_cols, levels_n, members, group = plan
    total = lat_n * lon_n
    packs = lon_n // group
    group_rows = group * share
    group_members = group_rows // levels_n
    slots_n, stencil = interp_ref.shape[2:4]
    lat, lon = lax.axis_index("lat"), lax.axis_index("lon")
    me = lat * lon_n + lon
    pack, place = lax.div(lon, group), lax.rem(lon, group)

    barrier = pltpu.get_barrier_semaphore()

    @pl.loop(1, total)
    def _(step):
        peer = lax.rem(me + step, total)
        pl.semaphore_signal(
            barrier,
            inc=1,
            device_id={"lat": peer // lon_n, "lon": lax.rem(peer, lon_n)},
            device_id_type=MESH,
        )

    pl.semaphore_wait(barrier, total - 1)

    def tile_copy(to_lat, to_lon, source):
        return pltpu.make_async_remote_copy(
            src_ref=ens_ref.at[
                :,
                pl.ds(pl.multiple_of(to_lat * tile_rows, tile_rows), tile_rows),
                pl.ds(pl.multiple_of(to_lon * tile_cols, tile_cols), tile_cols),
            ],
            dst_ref=state_ref.at[pl.ds(source * share, share)],
            send_sem=send_sem.at[to_lat * lon_n + to_lon],
            recv_sem=recv_sem.at[source],
            device_id={"lat": to_lat, "lon": to_lon},
            device_id_type=MESH,
        )

    def turn(t):
        far, step, g = lax.rem(t, 2), lax.rem(lax.div(t, 2), lat_n), lax.div(t, 2 * lat_n)
        back = lat_n - 1 - step
        turned = lax.div(g + packs - 1, packs) * (1 - far) + far
        by_lat = turned * back + (1 - turned) * step
        by_pack = far * (packs // 2) + g
        return flip(lat, by_lat, lat_n), flip(pack, by_pack, packs)

    own = pltpu.make_async_copy(
        ens_ref.at[
            :,
            pl.ds(pl.multiple_of(lat * tile_rows, tile_rows), tile_rows),
            pl.ds(pl.multiple_of(lon * tile_cols, tile_cols), tile_cols),
        ],
        state_ref.at[pl.ds(me * share, share)],
        recv_sem.at[me],
    )
    own.start()

    @pl.loop(0, lat_n * packs // 2)
    def _(step):
        @pl.loop(0, group)
        def _(i):
            for t in (step * 2 + 1, step * 2):
                to_lat, to_pack = turn(t)
                to_lon = to_pack * group + lax.rem(place + i, group)

                @pl.when(to_lat * lon_n + to_lon != me)
                def _():
                    tile_copy(to_lat, to_lon, me).start()

    loads = [
        pltpu.make_async_copy(source, target, load_sem.at[i])
        for i, (source, target) in enumerate(
            [
                (interp_in, interp_ref),
                (starts_in, starts_ref),
                (levels_in, levels_ref),
                (values_in, values_ref),
                (weights_in, weights_ref),
            ]
        )
    ]
    for copy in loads:
        copy.start()
    for copy in loads:
        copy.wait()

    last = lat_n - 1
    outside = pltpu.make_async_copy(nothing, slots_out.at[pl.ds(6, 3)], load_sem.at[2])

    @pl.when(lat == last)
    def _():
        nothing[...] = jnp.zeros_like(nothing)
        outside.start()

    cells = lax.broadcasted_iota(jnp.int32, (tile_cols, starts_ref.shape[-1]), 0)

    @pl.loop(0, slots_n, unroll=4)
    def _(j):
        first = starts_ref[0, 0, pl.ds(j, 1), :]
        taps = interp_ref[0, 0, j].astype(jnp.float32)
        offset = cells - first
        grid = jnp.zeros(cells.shape, jnp.float32)
        for p in range(stencil):
            grid = jnp.where(offset == p, taps[p : p + 1, :], grid)
        dense[j] = grid.astype(jnp.bfloat16)

    def hand_on(which):
        piece = pl.ds(which * group_rows, group_rows)
        return pltpu.make_async_copy(state_ref.at[piece], state_out.at[piece], hand_sem.at[which])

    def take_group(which):
        base = which * group_rows

        @pl.loop(0, group)
        def _(i):
            source = which * group + i
            tile_copy(source // lon_n, lax.rem(source, lon_n), source).wait_recv()

        hand_on(which).start()

        @pl.loop(0, group_members)
        def _(i):
            piece = state_ref[pl.ds(base + i * levels_n, levels_n)].astype(jnp.float32)
            span = levels_n * tile_rows
            wide[pl.ds(pl.multiple_of(i * span, span), span), :] = piece.reshape(span, tile_cols)

        for r in range(tile_rows):
            by_row[r] = wide[pl.ds(r, group_rows, stride=tile_rows), :].astype(jnp.bfloat16)

        first = which * group_members * (slots_n + 1)

        @pl.loop(0, slots_n, unroll=slots_n)
        def _(j):
            product = jnp.dot(by_row[rows_ref[j]], dense[j], preferred_element_type=jnp.float32)
            level = levels_ref[0, 0, j].astype(jnp.float32)
            obs[pl.ds(first + j, group_members, stride=slots_n + 1), :] = jnp.sum(
                product.reshape(group_members, levels_n, product.shape[1]) * level[None], axis=1
            )

    @pl.loop(0, lat_n * packs)
    def _(t):
        from_lat, from_pack = turn(t)
        take_group(from_lat * packs + from_pack)

    span, width = near.shape[1:]
    half = members // 2
    blank = jnp.zeros((width - members - half, tile_cols), jnp.float32)

    def add_blocks(pair, carry):
        lefts, rights = [], []
        for i in range(2):
            j = pair * 2 + i
            block = obs[pl.ds(j, members, stride=slots_n + 1), :]
            mean = jnp.sum(block, axis=0, keepdims=True) / members
            dev = block - mean
            innov = values_ref[0, 0, pl.ds(j, 1), :] - mean
            weight = weights_ref[0, 0, pl.ds(j, 1), :]
            live = jnp.where(jnp.full(weight.shape, j, jnp.int32) < count_ref[0], weight, 0.0)
            tail = jnp.broadcast_to(innov, (8, tile_cols))
            lefts.append(jnp.concatenate([dev, tail], axis=0).astype(jnp.bfloat16))
            heavy = dev * live
            rights.append(
                jnp.concatenate([heavy, heavy[half:], blank], axis=0).astype(jnp.bfloat16)
            )
        return carry + lax.dot_general(
            jnp.concatenate(lefts, axis=1),
            jnp.concatenate(rights, axis=1),
            (((1,), (1,)), ((), ())),
            preferred_element_type=jnp.float32,
        )

    summed = lax.fori_loop(
        0, slots_n // 2, add_blocks, jnp.zeros((members + 8, width), jnp.float32), unroll=slots_n // 2
    )
    lane = lax.broadcasted_iota(jnp.int32, (half, width), 1)
    near[1, :half] = jnp.where(lane < members, summed[:half], summed[half:members])
    near[1, half:] = summed[members:]

    def pass_on(source, target, sems, i, to_lat, to_lon):
        send, recv = sems
        return pltpu.make_async_remote_copy(
            src_ref=source,
            dst_ref=target,
            send_sem=send.at[i],
            recv_sem=recv.at[i],
            device_id={"lat": to_lat, "lon": to_lon},
            device_id_type=MESH,
        )

    east, west = lax.rem(lon + 1, lon_n), lax.rem(lon + lon_n - 1, lon_n)
    across = lax.rem(lon + lon_n // 2, lon_n)
    first, second = (near_send, near_recv), (slot_send, slot_recv)
    polar = (polar_send, polar_recv)
    row_mates = [
        pass_on(near.at[1], near.at[0], first, 0, lat, east),
        pass_on(near.at[1], near.at[2], first, 2, lat, west),
    ]
    over_pole = [
        pass_on(near.at[1], slots_out.at[s], polar, s, lat, lax.rem(across + lon_n + s - 1, lon_n))
        for s in range(3)
    ]
    south = pass_on(near, slots_out.at[pl.ds(0, 3)], second, 0, lat + 1, lon)
    north = pass_on(near, slots_out.at[pl.ds(6, 3)], second, 1, lat - 1, lon)
    keep_near = pltpu.make_async_copy(near, slots_out.at[pl.ds(3, 3)], load_sem.at[0])

    @pl.when(lat == 0)
    def _():
        for copy in over_pole:
            copy.start()

    for copy in row_mates:
        copy.start()

    for copy in row_mates:
        copy.wait_recv()

    @pl.when(lat < last)
    def _():
        south.start()

    @pl.when(lat > 0)
    def _():
        north.start()

    keep_near.start()

    @pl.loop(0, total)
    def _(peer):
        @pl.when(peer != me)
        def _():
            tile_copy(peer // lon_n, lax.rem(peer, lon_n), me).wait_send()

    @pl.loop(0, total // group)
    def _(which):
        hand_on(which).wait()

    for copy in row_mates:
        copy.wait_send()
    keep_near.wait()

    @pl.when(lat == 0)
    def _():
        for copy in over_pole:
            copy.wait()

    @pl.when(lat > 0)
    def _():
        south.wait_recv()
        north.wait_send()

    @pl.when(lat < last)
    def _():
        south.wait_send()
        north.wait_recv()

    @pl.when(lat == last)
    def _():
        outside.wait()


def halves(x):
    high = x.astype(jnp.bfloat16)
    return high, (x - high.astype(jnp.float32)).astype(jnp.bfloat16)


def stacked(first, second):
    return tuple(jnp.concatenate(pair, axis=0) for pair in zip(first, second))


def split_dot(left, right):
    left_high, left_low = left
    right_high, right_low = right
    members, width = right_high.shape
    blank = jnp.zeros((width - members, 2 * width), jnp.bfloat16)
    top = jnp.concatenate([right_high, right_low], axis=1)
    low = jnp.concatenate([right_high, jnp.zeros_like(right_low)], axis=1)
    out = jnp.dot(
        jnp.concatenate([left_high, left_low], axis=1),
        jnp.concatenate([top, blank, low, blank], axis=0),
        preferred_element_type=jnp.float32,
    )
    return out[:, :width] + out[:, width:]


def analysis_kernel(
    plan,
    state_in,
    slots_in,
    mask_in,
    out_ref,
    state,
    slots,
    mask,
    chosen,
    root,
    inverse,
    scales,
    target,
    stack,
    spots,
    big,
    dev,
    mean,
    result,
    state_sem,
    slot_sem,
    mask_sem,
    out_sem,
):
    members, levels_n, tile_rows, tile_cols, ns_iters = plan
    width = slots.shape[2]
    deep = members * tile_rows
    parts = ns_iters - 2
    per = levels_n // parts
    tiles = range(tile_rows)

    load_mask = pltpu.make_async_copy(mask_in, mask, mask_sem)
    load_mask.start()
    load_slots = pltpu.make_async_copy(slots_in, slots, slot_sem)
    load_slots.start()

    def load_state(i):
        piece = pl.ds(i * per, per)
        return pltpu.make_async_copy(state_in.at[:, piece], state.at[:, piece], state_sem.at[i])


    rows = lax.broadcasted_iota(jnp.int32, (members, width), 0)
    cols = lax.broadcasted_iota(jnp.int32, (members, width), 1)
    identity = jnp.where(rows == cols, 1.0, 0.0)
    source = lax.broadcasted_iota(jnp.int32, (width, deep), 0)
    spot = lax.broadcasted_iota(jnp.int32, (width, deep), 1) - source * tile_rows
    spots[...] = jnp.where((spot >= 0) & (spot < tile_rows), 1.0, 0.0).astype(jnp.bfloat16)

    load_mask.wait()
    use = mask[0, 0].astype(jnp.float32)
    for slot in range(9):
        chosen[slot] = jnp.broadcast_to(use[:, slot : slot + 1], chosen.shape[1:])

    load_slots.wait()
    for i in range(parts):
        load_state(i).start()

    half = members // 2
    lane = cols[:half]
    real = cols < members
    empty = jnp.zeros((width - half, width), jnp.float32)
    systems, totals = [], []
    for b in tiles:
        summed = chosen[0, b : b + 1] * slots[0]
        for slot in range(1, 9):
            summed += chosen[slot, b : b + 1] * slots[slot]
        target[b] = summed[half:]
        top = summed[:half]
        turned = pltpu.roll(top, width - half, 1)
        across = jnp.concatenate([turned, empty], axis=0).T[:half]
        bottom = jnp.where(lane < half, across, turned)
        whole = jnp.where(real, jnp.concatenate([top, bottom], axis=0), 0.0)
        system = (members - 1) * identity + whole
        totals.append(jnp.sum(system * system, axis=0, keepdims=True))
        systems.append(system)
    scale = jnp.sqrt(jnp.sum(jnp.concatenate(totals, axis=0), axis=1, keepdims=True))
    scales[...] = jnp.broadcast_to(scale, scales.shape)
    inverse_scale = 1.0 / scale
    def put(ref, b, pair):
        ref[b, 0], ref[b, 1] = pair

    def get(ref, b):
        return ref[b, 0], ref[b, 1]

    def advance(b, product, square, whole):
        cube = split_dot(halves(square), whole)
        return 2.25 * product - 1.5 * square + 0.25 * cube

    products = [systems[b] * inverse_scale[b : b + 1] for b in tiles]
    wholes = [halves(product) for product in products]
    squares = [split_dot(whole, whole) for whole in wholes]
    for b in tiles:
        inverse[b] = 1.5 * identity - 0.5 * products[b]
        root[b] = advance(b, products[b], squares[b], wholes[b])

    @pl.loop(0, parts, unroll=parts)
    def _(repeat):
        products = [root[b] for b in tiles]
        wholes = [halves(product) for product in products]
        squares, terms = [], []
        for b in tiles:
            both = stacked(wholes[b], halves(inverse[b]))
            out = split_dot(both, wholes[b])
            squares.append(out[:members])
            terms.append(out[members:])
        cubes = [split_dot(halves(squares[b]), wholes[b]) for b in tiles]
        load_state(repeat).wait()
        for i in range(per):
            f = repeat * per + i
            cell = state[:, f].astype(jnp.float32)
            average = jnp.sum(cell, axis=0) / members
            mean[f] = average
            dev[f] = (cell - average[None]).reshape(deep, tile_cols).astype(jnp.bfloat16)
        for b in tiles:
            inverse[b] = 1.5 * inverse[b] - 0.5 * terms[b]
            root[b] = 2.25 * products[b] - 1.5 * squares[b] + 0.25 * cubes[b]

    terms = []
    for b in tiles:
        term = inverse[b]
        terms.append(1.5 * term - 0.5 * split_dot(halves(term), halves(root[b])))
    scale = scales[...]
    root_scale = jnp.sqrt(jnp.float32(members - 1)) / jnp.sqrt(scale)
    inverse_scale = 1.0 / scale
    for b in tiles:
        half_step = jnp.sum(terms[b] * target[b][:1], axis=1, keepdims=True)
        shift = jnp.sum(terms[b] * half_step, axis=0, keepdims=True) * inverse_scale[b : b + 1]
        stack[pl.ds(b, members, stride=tile_rows), :] = terms[b] * root_scale[b : b + 1] + shift

    lane = lax.broadcasted_iota(jnp.int32, (tile_rows, tile_cols), 1)
    same = lax.rem(lane, tile_rows) == lax.broadcasted_iota(jnp.int32, lane.shape, 0)
    step = 128
    for first in range(0, deep, step):
        wide = jnp.dot(
            stack[first : first + step].astype(jnp.bfloat16),
            spots[...],
            preferred_element_type=jnp.float32,
        )
        for left in range(0, deep, tile_cols):
            block = wide[:, left : left + tile_cols].reshape(-1, tile_rows, tile_cols)
            big[first : first + step, left : left + tile_cols] = (
                jnp.where(same[None], block, 0.0).reshape(step, tile_cols).astype(jnp.bfloat16)
            )

    def send(pair):
        return pltpu.make_async_copy(
            result.at[:, pl.ds(pair * 2, 2)], out_ref.at[:, pl.ds(pair * 2, 2)], out_sem.at[pair]
        )

    @pl.loop(0, levels_n // 2, unroll=levels_n // 2)
    def _(pair):
        f = pair * 2
        right = jnp.concatenate([dev[f], dev[f + 1]], axis=1)
        update = jnp.dot(big[...], right, preferred_element_type=jnp.float32)
        for half in range(2):
            block = update[:, half * tile_cols : (half + 1) * tile_cols].reshape(
                members, tile_rows, tile_cols
            )
            result[:, f + half] = (block + mean[f + half][None]).astype(jnp.bfloat16)
        send(pair).start()

    @pl.loop(0, levels_n // 2)
    def _(pair):
        send(pair).wait()


def per_device(
    ensemble,
    obs_interp,
    obs_start,
    obs_levels,
    obs_values,
    obs_weight,
    obs_rows,
    obs_count,
    local_mask,
):
    lat_n = lax.axis_size("lat")
    lon_n = lax.axis_size("lon")
    total = lat_n * lon_n
    share, grid_rows, grid_cols = ensemble.shape
    tile_rows = grid_rows // lat_n
    tile_cols = grid_cols // lon_n
    slots_n, levels_n, obs_n = obs_levels.shape[2:]
    members = share * total // levels_n
    group = math.lcm(share, levels_n) // share
    groups = total // group
    span, width = members // 2 + 8, -(-members // 128) * 128
    plan = (lat_n, lon_n, share, tile_rows, tile_cols, levels_n, members, group)
    hbm = pl.BlockSpec(memory_space=pltpu.HBM)
    smem = pl.BlockSpec(memory_space=pltpu.SMEM)
    state, slots = pl.pallas_call(
        functools.partial(gather_kernel, plan),
        out_shape=(
            jax.ShapeDtypeStruct((share * total, tile_rows, tile_cols), jnp.bfloat16),
            jax.ShapeDtypeStruct((9, span, width), jnp.float32),
        ),
        in_specs=[hbm] * 6 + [smem] * 2,
        out_specs=(hbm, hbm),
        scratch_shapes=[pltpu.VMEM((share * total, tile_rows, tile_cols), jnp.bfloat16)]
        + [
            pltpu.VMEM(array.shape, array.dtype)
            for array in (obs_interp, obs_start, obs_levels, obs_values, obs_weight)
        ]
        + [
            pltpu.VMEM((slots_n, tile_cols, obs_n), jnp.bfloat16),
            pltpu.VMEM((tile_rows, group * share, tile_cols), jnp.bfloat16),
            pltpu.VMEM((group * share * tile_rows, tile_cols), jnp.float32),
            pltpu.VMEM((members * (slots_n + 1), obs_n), jnp.float32),
            pltpu.VMEM((3, span, width), jnp.float32),
            pltpu.VMEM((3, span, width), jnp.float32),
            pltpu.SemaphoreType.DMA((total,)),
            pltpu.SemaphoreType.DMA((total,)),
            pltpu.SemaphoreType.DMA((3,)),
            pltpu.SemaphoreType.DMA((3,)),
            pltpu.SemaphoreType.DMA((2,)),
            pltpu.SemaphoreType.DMA((2,)),
            pltpu.SemaphoreType.DMA((3,)),
            pltpu.SemaphoreType.DMA((3,)),
            pltpu.SemaphoreType.DMA((5,)),
            pltpu.SemaphoreType.DMA((groups,)),
        ],
        compiler_params=pltpu.CompilerParams(
            collective_id=0, has_side_effects=True, vmem_limit_bytes=60 * 1024 * 1024
        ),
    )(
        ensemble,
        obs_interp,
        obs_start,
        obs_levels,
        obs_values,
        obs_weight,
        obs_rows.reshape(-1),
        obs_count.reshape(-1),
    )
    tile_state = state.reshape(members, levels_n, tile_rows, tile_cols)
    deep = members * tile_rows
    pairs = (tile_rows, members, width)
    return pl.pallas_call(
        functools.partial(
            analysis_kernel, (members, levels_n, tile_rows, tile_cols, NS_ITERS)
        ),
        out_shape=jax.ShapeDtypeStruct(tile_state.shape, jnp.bfloat16),
        in_specs=[hbm, hbm, hbm],
        out_specs=hbm,
        scratch_shapes=[
            pltpu.VMEM(tile_state.shape, jnp.bfloat16),
            pltpu.VMEM(slots.shape, jnp.float32),
            pltpu.VMEM(local_mask.shape, jnp.int32),
            pltpu.VMEM((9, tile_rows, width), jnp.float32),
            pltpu.VMEM(pairs, jnp.float32),
            pltpu.VMEM(pairs, jnp.float32),
            pltpu.VMEM((tile_rows, width), jnp.float32),
            pltpu.VMEM((tile_rows, 8, width), jnp.float32),
            pltpu.VMEM((deep, width), jnp.float32),
            pltpu.VMEM((width, deep), jnp.bfloat16),
            pltpu.VMEM((deep, deep), jnp.bfloat16),
            pltpu.VMEM((levels_n, deep, tile_cols), jnp.bfloat16),
            pltpu.VMEM((levels_n, tile_rows, tile_cols), jnp.float32),
            pltpu.VMEM(tile_state.shape, jnp.bfloat16),
            pltpu.SemaphoreType.DMA((NS_ITERS - 2,)),
            pltpu.SemaphoreType.DMA,
            pltpu.SemaphoreType.DMA,
            pltpu.SemaphoreType.DMA((levels_n // 2,)),
        ],
        compiler_params=pltpu.CompilerParams(vmem_limit_bytes=60 * 1024 * 1024),
    )(tile_state, slots, local_mask)


def solution(mesh):
    placed = (
        P(("lat", "lon"), None, None),
        P("lat", "lon", None, None, None),
        P("lat", "lon", None, None),
        P("lat", "lon", None, None, None),
        P("lat", "lon", None, None),
        P("lat", "lon", None, None),
        P("lat", "lon", None),
        P("lat", "lon"),
        P("lat", "lon", None, None),
    )
    return jax.shard_map(
        per_device,
        mesh=mesh,
        in_specs=placed,
        out_specs=P(None, None, "lat", "lon"),
        check_vma=False,
    )
```

```python
import functools
import math

import jax
import jax.numpy as jnp
from jax import lax
from jax.experimental import pallas as pl
from jax.experimental.pallas import tpu as pltpu
from jax.sharding import PartitionSpec as P

NS_ITERS = 6
MESH = pl.DeviceIdType.MESH


def flip(index, by, size):
    total, bit = 0, 1
    while bit < size:
        total += lax.rem(lax.div(index, bit) + lax.div(by, bit), 2) * bit
        bit *= 2
    return total


def gather_kernel(
    plan,
    ens_ref,
    interp_in,
    starts_in,
    levels_in,
    values_in,
    weights_in,
    rows_ref,
    count_ref,
    state_out,
    slots_out,
    state_ref,
    interp_ref,
    starts_ref,
    levels_ref,
    values_ref,
    weights_ref,
    dense,
    by_row,
    wide,
    obs,
    near,
    nothing,
    send_sem,
    recv_sem,
    near_send,
    near_recv,
    slot_send,
    slot_recv,
    polar_send,
    polar_recv,
    load_sem,
    hand_sem,
):
    lat_n, lon_n, share, tile_rows, tile_cols, levels_n, members, group = plan
    total = lat_n * lon_n
    packs = lon_n // group
    group_rows = group * share
    group_members = group_rows // levels_n
    slots_n, stencil = interp_ref.shape[2:4]
    lat, lon = lax.axis_index("lat"), lax.axis_index("lon")
    me = lat * lon_n + lon
    pack, place = lax.div(lon, group), lax.rem(lon, group)

    barrier = pltpu.get_barrier_semaphore()

    @pl.loop(1, total)
    def _(step):
        peer = lax.rem(me + step, total)
        pl.semaphore_signal(
            barrier,
            inc=1,
            device_id={"lat": peer // lon_n, "lon": lax.rem(peer, lon_n)},
            device_id_type=MESH,
        )

    pl.semaphore_wait(barrier, total - 1)

    def tile_copy(to_lat, to_lon, source):
        return pltpu.make_async_remote_copy(
            src_ref=ens_ref.at[
                :,
                pl.ds(pl.multiple_of(to_lat * tile_rows, tile_rows), tile_rows),
                pl.ds(pl.multiple_of(to_lon * tile_cols, tile_cols), tile_cols),
            ],
            dst_ref=state_ref.at[pl.ds(source * share, share)],
            send_sem=send_sem.at[to_lat * lon_n + to_lon],
            recv_sem=recv_sem.at[source],
            device_id={"lat": to_lat, "lon": to_lon},
            device_id_type=MESH,
        )

    def turn(t):
        far, step, g = lax.rem(t, 2), lax.rem(lax.div(t, 2), lat_n), lax.div(t, 2 * lat_n)
        back = lat_n - 1 - step
        turned = lax.div(g + packs - 1, packs) * (1 - far) + far
        by_lat = turned * back + (1 - turned) * step
        by_pack = far * (packs // 2) + g
        return flip(lat, by_lat, lat_n), flip(pack, by_pack, packs)

    own = pltpu.make_async_copy(
        ens_ref.at[
            :,
            pl.ds(pl.multiple_of(lat * tile_rows, tile_rows), tile_rows),
            pl.ds(pl.multiple_of(lon * tile_cols, tile_cols), tile_cols),
        ],
        state_ref.at[pl.ds(me * share, share)],
        recv_sem.at[me],
    )
    own.start()

    @pl.loop(0, lat_n * packs // 2)
    def _(step):
        @pl.loop(0, group)
        def _(i):
            for t in (step * 2 + 1, step * 2):
                to_lat, to_pack = turn(t)
                to_lon = to_pack * group + lax.rem(place + i, group)

                @pl.when(to_lat * lon_n + to_lon != me)
                def _():
                    tile_copy(to_lat, to_lon, me).start()

    loads = [
        pltpu.make_async_copy(source, target, load_sem.at[i])
        for i, (source, target) in enumerate(
            [
                (interp_in, interp_ref),
                (starts_in, starts_ref),
                (levels_in, levels_ref),
                (values_in, values_ref),
                (weights_in, weights_ref),
            ]
        )
    ]
    for copy in loads:
        copy.start()
    for copy in loads:
        copy.wait()

    last = lat_n - 1
    outside = pltpu.make_async_copy(nothing, slots_out.at[pl.ds(6, 3)], load_sem.at[2])

    @pl.when(lat == last)
    def _():
        nothing[...] = jnp.zeros_like(nothing)
        outside.start()

    cells = lax.broadcasted_iota(jnp.int32, (tile_cols, starts_ref.shape[-1]), 0)

    @pl.loop(0, slots_n, unroll=4)
    def _(j):
        first = starts_ref[0, 0, pl.ds(j, 1), :]
        taps = interp_ref[0, 0, j].astype(jnp.float32)
        offset = cells - first
        grid = jnp.zeros(cells.shape, jnp.float32)
        for p in range(stencil):
            grid = jnp.where(offset == p, taps[p : p + 1, :], grid)
        dense[j] = grid.astype(jnp.bfloat16)

    def hand_on(which):
        piece = pl.ds(which * group_rows, group_rows)
        return pltpu.make_async_copy(state_ref.at[piece], state_out.at[piece], hand_sem.at[which])

    def take_group(which):
        base = which * group_rows

        @pl.loop(0, group)
        def _(i):
            source = which * group + i
            tile_copy(source // lon_n, lax.rem(source, lon_n), source).wait_recv()

        hand_on(which).start()

        @pl.loop(0, group_members)
        def _(i):
            piece = state_ref[pl.ds(base + i * levels_n, levels_n)].astype(jnp.float32)
            span = levels_n * tile_rows
            wide[pl.ds(pl.multiple_of(i * span, span), span), :] = piece.reshape(span, tile_cols)

        for r in range(tile_rows):
            by_row[r] = wide[pl.ds(r, group_rows, stride=tile_rows), :].astype(jnp.bfloat16)

        first = which * group_members * (slots_n + 1)

        @pl.loop(0, slots_n, unroll=slots_n)
        def _(j):
            product = jnp.dot(by_row[rows_ref[j]], dense[j], preferred_element_type=jnp.float32)
            level = levels_ref[0, 0, j].astype(jnp.float32)
            obs[pl.ds(first + j, group_members, stride=slots_n + 1), :] = jnp.sum(
                product.reshape(group_members, levels_n, product.shape[1]) * level[None], axis=1
            )

    @pl.loop(0, lat_n * packs)
    def _(t):
        from_lat, from_pack = turn(t)
        take_group(from_lat * packs + from_pack)

    span, width = near.shape[1:]
    half = members // 2
    blank = jnp.zeros((width - members - half, tile_cols), jnp.float32)

    def add_blocks(pair, carry):
        lefts, rights = [], []
        for i in range(2):
            j = pair * 2 + i
            block = obs[pl.ds(j, members, stride=slots_n + 1), :]
            mean = jnp.sum(block, axis=0, keepdims=True) / members
            dev = block - mean
            innov = values_ref[0, 0, pl.ds(j, 1), :] - mean
            weight = weights_ref[0, 0, pl.ds(j, 1), :]
            live = jnp.where(jnp.full(weight.shape, j, jnp.int32) < count_ref[0], weight, 0.0)
            tail = jnp.broadcast_to(innov, (8, tile_cols))
            lefts.append(jnp.concatenate([dev, tail], axis=0).astype(jnp.bfloat16))
            heavy = dev * live
            rights.append(
                jnp.concatenate([heavy, heavy[half:], blank], axis=0).astype(jnp.bfloat16)
            )
        return carry + lax.dot_general(
            jnp.concatenate(lefts, axis=1),
            jnp.concatenate(rights, axis=1),
            (((1,), (1,)), ((), ())),
            preferred_element_type=jnp.float32,
        )

    summed = lax.fori_loop(
        0, slots_n // 2, add_blocks, jnp.zeros((members + 8, width), jnp.float32), unroll=slots_n // 2
    )
    lane = lax.broadcasted_iota(jnp.int32, (half, width), 1)
    near[1, :half] = jnp.where(lane < members, summed[:half], summed[half:members])
    near[1, half:] = summed[members:]

    def pass_on(source, target, sems, i, to_lat, to_lon):
        send, recv = sems
        return pltpu.make_async_remote_copy(
            src_ref=source,
            dst_ref=target,
            send_sem=send.at[i],
            recv_sem=recv.at[i],
            device_id={"lat": to_lat, "lon": to_lon},
            device_id_type=MESH,
        )

    east, west = lax.rem(lon + 1, lon_n), lax.rem(lon + lon_n - 1, lon_n)
    across = lax.rem(lon + lon_n // 2, lon_n)
    first, second = (near_send, near_recv), (slot_send, slot_recv)
    polar = (polar_send, polar_recv)
    row_mates = [
        pass_on(near.at[1], near.at[0], first, 0, lat, east),
        pass_on(near.at[1], near.at[2], first, 2, lat, west),
    ]
    over_pole = [
        pass_on(near.at[1], slots_out.at[s], polar, s, lat, lax.rem(across + lon_n + s - 1, lon_n))
        for s in range(3)
    ]
    south = pass_on(near, slots_out.at[pl.ds(0, 3)], second, 0, lat + 1, lon)
    north = pass_on(near, slots_out.at[pl.ds(6, 3)], second, 1, lat - 1, lon)
    keep_near = pltpu.make_async_copy(near, slots_out.at[pl.ds(3, 3)], load_sem.at[0])

    @pl.when(lat == 0)
    def _():
        for copy in over_pole:
            copy.start()

    for copy in row_mates:
        copy.start()

    for copy in row_mates:
        copy.wait_recv()

    @pl.when(lat < last)
    def _():
        south.start()

    @pl.when(lat > 0)
    def _():
        north.start()

    keep_near.start()

    @pl.loop(0, total)
    def _(peer):
        @pl.when(peer != me)
        def _():
            tile_copy(peer // lon_n, lax.rem(peer, lon_n), me).wait_send()

    @pl.loop(0, total // group)
    def _(which):
        hand_on(which).wait()

    for copy in row_mates:
        copy.wait_send()
    keep_near.wait()

    @pl.when(lat == 0)
    def _():
        for copy in over_pole:
            copy.wait()

    @pl.when(lat > 0)
    def _():
        south.wait_recv()
        north.wait_send()

    @pl.when(lat < last)
    def _():
        south.wait_send()
        north.wait_recv()

    @pl.when(lat == last)
    def _():
        outside.wait()


def halves(x):
    high = x.astype(jnp.bfloat16)
    return high, (x - high.astype(jnp.float32)).astype(jnp.bfloat16)


def stacked(first, second):
    return tuple(jnp.concatenate(pair, axis=0) for pair in zip(first, second))


def split_dot(left, right):
    left_high, left_low = left
    right_high, right_low = right
    members, width = right_high.shape
    blank = jnp.zeros((width - members, 2 * width), jnp.bfloat16)
    top = jnp.concatenate([right_high, right_low], axis=1)
    low = jnp.concatenate([right_high, jnp.zeros_like(right_low)], axis=1)
    out = jnp.dot(
        jnp.concatenate([left_high, left_low], axis=1),
        jnp.concatenate([top, blank, low, blank], axis=0),
        preferred_element_type=jnp.float32,
    )
    return out[:, :width] + out[:, width:]


def analysis_kernel(
    plan,
    state_in,
    slots_in,
    mask_in,
    out_ref,
    state,
    slots,
    mask,
    chosen,
    root,
    inverse,
    scales,
    target,
    stack,
    spots,
    big,
    dev,
    mean,
    result,
    state_sem,
    slot_sem,
    mask_sem,
    out_sem,
):
    members, levels_n, tile_rows, tile_cols, ns_iters = plan
    width = slots.shape[2]
    deep = members * tile_rows
    parts = ns_iters - 2
    per = levels_n // parts
    tiles = range(tile_rows)

    load_mask = pltpu.make_async_copy(mask_in, mask, mask_sem)
    load_mask.start()
    load_slots = pltpu.make_async_copy(slots_in, slots, slot_sem)
    load_slots.start()

    def load_state(i):
        piece = pl.ds(i * per, per)
        return pltpu.make_async_copy(state_in.at[:, piece], state.at[:, piece], state_sem.at[i])


    rows = lax.broadcasted_iota(jnp.int32, (members, width), 0)
    cols = lax.broadcasted_iota(jnp.int32, (members, width), 1)
    identity = jnp.where(rows == cols, 1.0, 0.0)
    source = lax.broadcasted_iota(jnp.int32, (width, deep), 0)
    spot = lax.broadcasted_iota(jnp.int32, (width, deep), 1) - source * tile_rows
    spots[...] = jnp.where((spot >= 0) & (spot < tile_rows), 1.0, 0.0).astype(jnp.bfloat16)

    load_mask.wait()
    use = mask[0, 0].astype(jnp.float32)
    for slot in range(9):
        chosen[slot] = jnp.broadcast_to(use[:, slot : slot + 1], chosen.shape[1:])

    load_slots.wait()
    for i in range(parts):
        load_state(i).start()

    half = members // 2
    lane = cols[:half]
    real = cols < members
    empty = jnp.zeros((width - half, width), jnp.float32)
    systems, totals = [], []
    for b in tiles:
        summed = chosen[0, b : b + 1] * slots[0]
        for slot in range(1, 9):
            summed += chosen[slot, b : b + 1] * slots[slot]
        target[b] = summed[half:]
        top = summed[:half]
        turned = pltpu.roll(top, width - half, 1)
        across = jnp.concatenate([turned, empty], axis=0).T[:half]
        bottom = jnp.where(lane < half, across, turned)
        whole = jnp.where(real, jnp.concatenate([top, bottom], axis=0), 0.0)
        system = (members - 1) * identity + whole
        totals.append(jnp.sum(system * system, axis=0, keepdims=True))
        systems.append(system)
    scale = jnp.sqrt(jnp.sum(jnp.concatenate(totals, axis=0), axis=1, keepdims=True))
    scales[...] = jnp.broadcast_to(scale, scales.shape)
    inverse_scale = 1.0 / scale
    def put(ref, b, pair):
        ref[b, 0], ref[b, 1] = pair

    def get(ref, b):
        return ref[b, 0], ref[b, 1]

    def advance(b, product, square, whole):
        cube = split_dot(halves(square), whole)
        return 2.25 * product - 1.5 * square + 0.25 * cube

    products = [systems[b] * inverse_scale[b : b + 1] for b in tiles]
    wholes = [halves(product) for product in products]
    squares = [split_dot(whole, whole) for whole in wholes]
    for b in tiles:
        inverse[b] = 1.5 * identity - 0.5 * products[b]
        root[b] = advance(b, products[b], squares[b], wholes[b])

    @pl.loop(0, parts, unroll=parts)
    def _(repeat):
        products = [root[b] for b in tiles]
        wholes = [halves(product) for product in products]
        squares, terms = [], []
        for b in tiles:
            both = stacked(wholes[b], halves(inverse[b]))
            out = split_dot(both, wholes[b])
            squares.append(out[:members])
            terms.append(out[members:])
        cubes = [split_dot(halves(squares[b]), wholes[b]) for b in tiles]
        load_state(repeat).wait()
        for i in range(per):
            f = repeat * per + i
            cell = state[:, f].astype(jnp.float32)
            average = jnp.sum(cell, axis=0) / members
            mean[f] = average
            dev[f] = (cell - average[None]).reshape(deep, tile_cols).astype(jnp.bfloat16)
        for b in tiles:
            inverse[b] = 1.5 * inverse[b] - 0.5 * terms[b]
            root[b] = 2.25 * products[b] - 1.5 * squares[b] + 0.25 * cubes[b]

    terms = []
    for b in tiles:
        term = inverse[b]
        terms.append(1.5 * term - 0.5 * split_dot(halves(term), halves(root[b])))
    scale = scales[...]
    root_scale = jnp.sqrt(jnp.float32(members - 1)) / jnp.sqrt(scale)
    inverse_scale = 1.0 / scale
    for b in tiles:
        half_step = jnp.sum(terms[b] * target[b][:1], axis=1, keepdims=True)
        shift = jnp.sum(terms[b] * half_step, axis=0, keepdims=True) * inverse_scale[b : b + 1]
        stack[pl.ds(b, members, stride=tile_rows), :] = terms[b] * root_scale[b : b + 1] + shift

    lane = lax.broadcasted_iota(jnp.int32, (tile_rows, tile_cols), 1)
    same = lax.rem(lane, tile_rows) == lax.broadcasted_iota(jnp.int32, lane.shape, 0)
    step = 128
    for first in range(0, deep, step):
        wide = jnp.dot(
            stack[first : first + step].astype(jnp.bfloat16),
            spots[...],
            preferred_element_type=jnp.float32,
        )
        for left in range(0, deep, tile_cols):
            block = wide[:, left : left + tile_cols].reshape(-1, tile_rows, tile_cols)
            big[first : first + step, left : left + tile_cols] = (
                jnp.where(same[None], block, 0.0).reshape(step, tile_cols).astype(jnp.bfloat16)
            )

    def send(pair):
        return pltpu.make_async_copy(
            result.at[:, pl.ds(pair * 2, 2)], out_ref.at[:, pl.ds(pair * 2, 2)], out_sem.at[pair]
        )

    @pl.loop(0, levels_n // 2, unroll=levels_n // 2)
    def _(pair):
        f = pair * 2
        right = jnp.concatenate([dev[f], dev[f + 1]], axis=1)
        for first in range(0, deep, deep // 2):
            update = jnp.dot(big[first : first + deep // 2], right, preferred_element_type=jnp.float32)
            some = slice(first // tile_rows, (first + deep // 2) // tile_rows)
            for half in range(2):
                block = update[:, half * tile_cols : (half + 1) * tile_cols].reshape(
                    -1, tile_rows, tile_cols
                )
                result[some, f + half] = (block + mean[f + half][None]).astype(jnp.bfloat16)
        send(pair).start()

    @pl.loop(0, levels_n // 2)
    def _(pair):
        send(pair).wait()


def per_device(
    ensemble,
    obs_interp,
    obs_start,
    obs_levels,
    obs_values,
    obs_weight,
    obs_rows,
    obs_count,
    local_mask,
):
    lat_n = lax.axis_size("lat")
    lon_n = lax.axis_size("lon")
    total = lat_n * lon_n
    share, grid_rows, grid_cols = ensemble.shape
    tile_rows = grid_rows // lat_n
    tile_cols = grid_cols // lon_n
    slots_n, levels_n, obs_n = obs_levels.shape[2:]
    members = share * total // levels_n
    group = math.lcm(share, levels_n) // share
    groups = total // group
    span, width = members // 2 + 8, -(-members // 128) * 128
    plan = (lat_n, lon_n, share, tile_rows, tile_cols, levels_n, members, group)
    hbm = pl.BlockSpec(memory_space=pltpu.HBM)
    smem = pl.BlockSpec(memory_space=pltpu.SMEM)
    state, slots = pl.pallas_call(
        functools.partial(gather_kernel, plan),
        out_shape=(
            jax.ShapeDtypeStruct((share * total, tile_rows, tile_cols), jnp.bfloat16),
            jax.ShapeDtypeStruct((9, span, width), jnp.float32),
        ),
        in_specs=[hbm] * 6 + [smem] * 2,
        out_specs=(hbm, hbm),
        scratch_shapes=[pltpu.VMEM((share * total, tile_rows, tile_cols), jnp.bfloat16)]
        + [
            pltpu.VMEM(array.shape, array.dtype)
            for array in (obs_interp, obs_start, obs_levels, obs_values, obs_weight)
        ]
        + [
            pltpu.VMEM((slots_n, tile_cols, obs_n), jnp.bfloat16),
            pltpu.VMEM((tile_rows, group * share, tile_cols), jnp.bfloat16),
            pltpu.VMEM((group * share * tile_rows, tile_cols), jnp.float32),
            pltpu.VMEM((members * (slots_n + 1), obs_n), jnp.float32),
            pltpu.VMEM((3, span, width), jnp.float32),
            pltpu.VMEM((3, span, width), jnp.float32),
            pltpu.SemaphoreType.DMA((total,)),
            pltpu.SemaphoreType.DMA((total,)),
            pltpu.SemaphoreType.DMA((3,)),
            pltpu.SemaphoreType.DMA((3,)),
            pltpu.SemaphoreType.DMA((2,)),
            pltpu.SemaphoreType.DMA((2,)),
            pltpu.SemaphoreType.DMA((3,)),
            pltpu.SemaphoreType.DMA((3,)),
            pltpu.SemaphoreType.DMA((5,)),
            pltpu.SemaphoreType.DMA((groups,)),
        ],
        compiler_params=pltpu.CompilerParams(
            collective_id=0, has_side_effects=True, vmem_limit_bytes=60 * 1024 * 1024
        ),
    )(
        ensemble,
        obs_interp,
        obs_start,
        obs_levels,
        obs_values,
        obs_weight,
        obs_rows.reshape(-1),
        obs_count.reshape(-1),
    )
    tile_state = state.reshape(members, levels_n, tile_rows, tile_cols)
    deep = members * tile_rows
    pairs = (tile_rows, members, width)
    return pl.pallas_call(
        functools.partial(
            analysis_kernel, (members, levels_n, tile_rows, tile_cols, NS_ITERS)
        ),
        out_shape=jax.ShapeDtypeStruct(tile_state.shape, jnp.bfloat16),
        in_specs=[hbm, hbm, hbm],
        out_specs=hbm,
        scratch_shapes=[
            pltpu.VMEM(tile_state.shape, jnp.bfloat16),
            pltpu.VMEM(slots.shape, jnp.float32),
            pltpu.VMEM(local_mask.shape, jnp.int32),
            pltpu.VMEM((9, tile_rows, width), jnp.float32),
            pltpu.VMEM(pairs, jnp.float32),
            pltpu.VMEM(pairs, jnp.float32),
            pltpu.VMEM((tile_rows, width), jnp.float32),
            pltpu.VMEM((tile_rows, 8, width), jnp.float32),
            pltpu.VMEM((deep, width), jnp.float32),
            pltpu.VMEM((width, deep), jnp.bfloat16),
            pltpu.VMEM((deep, deep), jnp.bfloat16),
            pltpu.VMEM((levels_n, deep, tile_cols), jnp.bfloat16),
            pltpu.VMEM((levels_n, tile_rows, tile_cols), jnp.float32),
            pltpu.VMEM(tile_state.shape, jnp.bfloat16),
            pltpu.SemaphoreType.DMA((NS_ITERS - 2,)),
            pltpu.SemaphoreType.DMA,
            pltpu.SemaphoreType.DMA,
            pltpu.SemaphoreType.DMA((levels_n // 2,)),
        ],
        compiler_params=pltpu.CompilerParams(vmem_limit_bytes=60 * 1024 * 1024),
    )(tile_state, slots, local_mask)


def solution(mesh):
    placed = (
        P(("lat", "lon"), None, None),
        P("lat", "lon", None, None, None),
        P("lat", "lon", None, None),
        P("lat", "lon", None, None, None),
        P("lat", "lon", None, None),
        P("lat", "lon", None, None),
        P("lat", "lon", None),
        P("lat", "lon"),
        P("lat", "lon", None, None),
    )
    return jax.shard_map(
        per_device,
        mesh=mesh,
        in_specs=placed,
        out_specs=P(None, None, "lat", "lon"),
        check_vma=False,
    )
```
